32 devices in a mesh: tm: 2 (over core), space: 16 (over z, y, x).
Axes of the slice: x: 2, y: 2, z: 4, core: 2. Of those that a mesh axis runs over, the one named last changes fastest.
Arguments:
- slab_starts: float32 [2, 64, 24, 512], P('tm', 'space'), may hold values from -6 to 6
- forcing: float32 [2, 2, 64, 24, 512], P('tm', None, 'space'), may hold values from -5 to 5
- density: float32 [64, 24, 512], P('space'), may hold values from 0.25 to 4
- moving_flags: int32 [64, 24, 512], P('space'), may hold values 0 or 1
Outputs:
- new_starts: float32 [2, 64, 24, 512], P('tm', 'space')
- new_interior: float32 [2, 64, 24, 512], P('tm', 'space')
The draws below stay inside these ranges and needn't reach their ends.
All inputs are finite; a program needn't handle non-finite values. No bound on the sum of `moving_flags` on one device may be relied on, other than what follows from the above.
Results may differ from the reference program's by a relative error of at most 0.0001.
Values sent between devices are 32-bit elements; how exact they have to be, the bound alone decides.
A program may use at most 64 MiB of HBM per device.

```python
import math
import jax
import jax.numpy as jnp
from jax import lax

NY = 24
NZ = 512
STEPS = 2
VCYCLES = 1
COARSE_SWEEPS = 4
SLABS = 2
NX = 64


def draw_forcing(key, part):
    shape = (SLABS, STEPS, NX, NY, NZ)
    values = jnp.clip(jax.random.normal(key, shape, jnp.float32), -5.0, 5.0)
    return values


def plant(result, key, low, top_value):
    spot = [jax.random.randint(jax.random.fold_in(key, axis), (), 0, length) for axis, length in enumerate(result.shape)]
    main_axis = result.shape.index(max(result.shape))
    next_to = spot[:main_axis] + [(spot[main_axis] + 1) % result.shape[main_axis]] + spot[main_axis + 1:]
    return result.at[tuple(spot)].set(low).at[tuple(next_to)].set(top_value)


def block_scale(rng, dims, pieces, smallest, largest):
    gain, own = 1.0, jax.random.fold_in(rng, 6)
    for dim, parts in pieces:
        steps = jnp.exp(jax.random.uniform(jax.random.fold_in(own, dim), (parts,), jnp.float32, smallest / len(pieces), largest / len(pieces)))
        gain = gain * jnp.repeat(steps, dims[dim] // parts).reshape([-1 if axis == dim else 1 for axis in range(len(dims))])
    return gain


def gaussian(stream_key, dims, scale, limit, shards=(), held_as=jnp.bfloat16):
    array = jax.random.normal(stream_key, dims, jnp.float32) * scale
    if len(shards) > 0:
        array = block_scale(stream_key, dims, shards, -0.22, 0.18) * array
    return jnp.clip(array, min=-limit, max=limit).astype(held_as)


def setup_inputs(seed: int = 0) -> dict:
    key_of = jax.random.split(jax.random.key(seed), 5)
    slab_starts = gaussian(key_of[0], (SLABS, NX, NY, NZ), 1.0, 6.0, ((0, 2), (1, 16)), jnp.float32)
    forcing = draw_forcing(jax.random.fold_in(key_of[4], 71), 0)
    density = jnp.clip(jnp.exp(math.log(4.0) - 2.7725887 * jax.random.uniform(key_of[2], (NX, NY, NZ), jnp.float32) ** block_scale(key_of[2], (NX, NY, NZ), ((0, 16),), -0.2, 0.2)), 0.25, 4.0)
    moving_flags = plant((jax.random.randint(key_of[3], (NX, NY, NZ), 0, 4) < 1).astype(jnp.int32), jax.random.fold_in(key_of[3], 1), 0, 1)
    return dict(slab_starts=slab_starts, forcing=forcing, density=density, moving_flags=moving_flags)


STIFFNESS = 4.0
COARSE_STIFF = 0.25
FORCE_WEIGHT = 0.5
RELAX = 0.8
MASS_FLAG = 3.0


def shrink(field):
    a, b, c = field.shape
    return field.reshape(a // 2, 2, b // 2, 2, c // 2, 2).mean(axis=(1, 3, 5))


def expand(field):
    return jnp.repeat(jnp.repeat(jnp.repeat(field, 2, axis=0), 2, axis=1), 2, axis=2)


def neighbour_sum(field):
    padded = jnp.pad(field, 1)
    total = padded[2:, 1:-1, 1:-1] + padded[:-2, 1:-1, 1:-1]
    total = total + padded[1:-1, 2:, 1:-1] + padded[1:-1, :-2, 1:-1]
    return total + padded[1:-1, 1:-1, 2:] + padded[1:-1, 1:-1, :-2]


def operate(field, mass, conduct, stiff):
    return mass * field + stiff * conduct * (6.0 * field - neighbour_sum(field))


def advance(prior, source, mass, conduct, mass_c, conduct_c):
    rhs = mass * prior + FORCE_WEIGHT * source
    diag = mass + 6.0 * STIFFNESS * conduct
    diag_c = mass_c + 6.0 * COARSE_STIFF * conduct_c
    state = prior
    for cycle in range(VCYCLES):
        state = state + RELAX * (rhs - operate(state, mass, conduct, STIFFNESS)) / diag
        resid = rhs - operate(state, mass, conduct, STIFFNESS)
        coarse_rhs = shrink(shrink(resid))
        error = RELAX * coarse_rhs / diag_c
        for sweep in range(COARSE_SWEEPS - 1):
            error = error + RELAX * (coarse_rhs - operate(error, mass_c, conduct_c, COARSE_STIFF)) / diag_c
        state = state + expand(expand(error))
    return state


def reference(slab_starts, forcing, density, moving_flags):
    conduct = 1.0 / density
    mass = 1.0 + MASS_FLAG * moving_flags.astype(jnp.float32)
    mass_c = shrink(shrink(mass))
    conduct_c = shrink(shrink(conduct))

    def whole_slab(pair):
        start, source = pair
        middle = advance(start, source[0], mass, conduct, mass_c, conduct_c)
        return advance(middle, source[1], mass, conduct, mass_c, conduct_c)

    ends = lax.map(whole_slab, (slab_starts, forcing))
    new_starts = jnp.roll(ends, 1, axis=0)

    def first_step(pair):
        return advance(pair[0], pair[1][0], mass, conduct, mass_c, conduct_c)

    new_interior = lax.map(first_step, (new_starts, forcing))
    return (new_starts, new_interior)
```

```python
import functools

import jax
import jax.numpy as jnp
from jax import lax
from jax.experimental import pallas as pl
from jax.experimental.pallas import tpu as pltpu
from jax.sharding import PartitionSpec as P

COARSE_SWEEPS = 4
STIFFNESS = 4.0
COARSE_STIFF = 0.25
FORCE_WEIGHT = 0.5
RELAX = 0.8
MASS_FLAG = 3.0

MESH = pl.DeviceIdType.MESH
REACH = COARSE_SWEEPS
SLOTS = 2 * REACH + 1
FAR = REACH + 1
F32 = jnp.float32
BF16 = jnp.bfloat16

FACES = ("xm", "xp", "ym", "yp", "zm", "zp")
EDGES = [(f, d) for i, f in enumerate(FACES) for d in FACES[i + 1:] if f[0] != d[0]]
POINTS = ["0"] + list(FACES) + [f + d for f, d in EDGES]

OWN = ["V0", "V3", "V"] + [f + s for f in ("ym", "yp", "zm", "zp") for s in ("0", "3", "")]
BESIDE = ["xm", "xp"]
SUMS = OWN + BESIDE


def split(x):
    hi = x.astype(BF16).astype(F32)
    return [hi, (x - hi).astype(BF16).astype(F32)]


def kernel(
    n, nt, planes,
    starts, forcing, density, flags, out_base, out_state, base_shift, state_shift,
    p0, u0, b1, u1, came, v2, force, rho, moving, stiff, diag, alpha, beta, hard,
    part_in, part_out, ring, own, cross, cross_out, gam, soft, coarse_rows, sums, operator, wide, narrow, spread, sizes,
    load_sem, send_sem, recv_sem,
):
    t = lax.axis_index("tm")
    me = lax.axis_index("space")
    ahead, behind = lax.rem(t + 1, nt), lax.rem(t + nt - 1, nt)
    half = lax.rem(t, 2)
    mate = t + 1 - 2 * half
    top = planes + 2
    last = planes - 1
    ny, nz = p0.shape[-2:]
    ncy, ncz = 8, nz // 4
    mine = pl.ds(pl.multiple_of(half * (nz // 2), nz // 2), nz // 2)
    theirs = pl.ds(pl.multiple_of((1 - half) * (nz // 2), nz // 2), nz // 2)

    def inside(offset):
        if offset < 0:
            return me >= -offset
        return me < n - offset

    order = [1, -1, 3, -3, 2, -2, 4, -4]

    barrier = pltpu.get_barrier_semaphore()
    for d in (1, -1, 2, -2, 3, -3, 4, -4):
        @pl.when(inside(d))
        def _(d=d):
            pl.semaphore_signal(barrier, inc=1, device_id=(t, me + d), device_id_type=MESH)
            pl.semaphore_signal(barrier, inc=1, device_id=(behind, me + d), device_id_type=MESH)
    pl.semaphore_signal(barrier, inc=1, device_id=(behind, me), device_id_type=MESH)
    pl.semaphore_signal(barrier, inc=1, device_id=(ahead, me), device_id_type=MESH)

    fine = ny * nz // 128
    coarse = ncy

    def finish(semaphore, rows):
        whole = sizes.at[pl.ds(0, rows)]
        pltpu.make_async_copy(whole, whole, semaphore).wait()

    for src, dst in (
        (density, rho), (flags, moving), (starts.at[0], p0.at[pl.ds(2, planes)]), (forcing.at[0], force),
    ):
        pltpu.make_async_copy(src, dst, load_sem).start()

    first, passed, part, stiffs, stiffs_passed, bases = [[2 * j, 2 * j + 1] for j in range(6)]
    states = 12
    near = {d: 13 + j for j, d in enumerate(d for d in range(-REACH, REACH + 1) if d != 0)}
    around_next = {d: 21 + j for j, d in enumerate(range(-FAR, FAR + 1))}
    late = {d: 32 + j for j, d in enumerate(d for d in range(-REACH, REACH + 1) if d != 0)}
    sent = dict.fromkeys(range(-FAR, FAR + 1), 0)

    def when_inside(offset, act):
        if offset == 0:
            act()
        else:
            pl.when(inside(offset))(act)

    def send(src, dst, k, rows, offset, tm, to=None):
        copy = pltpu.make_async_remote_copy(
            src_ref=src, dst_ref=dst, send_sem=send_sem.at[offset + FAR], recv_sem=recv_sem.at[k],
            device_id=(tm, me + offset if to is None else to), device_id_type=MESH,
        )
        when_inside(offset, lambda: copy.start())
        sent[offset] += rows

    def receive(k, rows, offset):
        when_inside(offset, lambda: finish(recv_sem.at[k], rows))

    for d in range(-REACH, REACH + 1):
        if d == 0:
            continue

        @pl.when(jnp.logical_not(inside(d)))
        def _(d=d):
            zero = jnp.zeros((ncy, ncz), F32)
            gam[REACH + d] = zero
            for step in range(3):
                ring[step, REACH + d] = zero
            if abs(d) == 1:
                side = 0 if d < 0 else 1
                fine_zero = jnp.zeros((ny, nz), F32)
                edge = 1 if d < 0 else top
                p0[edge] = fine_zero
                b1[edge] = fine_zero
                beta[edge] = fine_zero
                hard[side] = fine_zero
                part_in[side] = fine_zero
                soft[side] = zero

    for d in range(-FAR, FAR + 1):
        if d == 0:
            continue

        @pl.when(jnp.logical_not(inside(d)))
        def _(d=d):
            zero = jnp.zeros((ncy, ncz), F32)
            for step in range(2):
                for side in range(2):
                    cross[step, FAR + d, side] = zero

    lane_of = lax.broadcasted_iota(jnp.int32, (nz, ncz), 0)
    block_of = lax.broadcasted_iota(jnp.int32, (nz, ncz), 1)
    for j, pick in enumerate([
        lane_of // 4 == block_of, lane_of == 4 * block_of, lane_of == 4 * block_of + 3,
    ]):
        narrow[:, j * ncz:(j + 1) * ncz] = pick.astype(F32).astype(BF16)
    one = (
        lax.broadcasted_iota(jnp.int32, (ncz, nz), 1) // 4 == lax.broadcasted_iota(jnp.int32, (ncz, nz), 0)
    ).astype(F32).astype(BF16)
    for piece in range(2):
        wide[pl.ds(piece * ncz, ncz), :] = one
    coarse_rows[...] = jnp.zeros_like(coarse_rows)
    for j in range(len(SUMS)):
        for cols in range(3):
            sums[j, cols, pl.ds(ny, 8), :] = jnp.zeros((8, ncz), F32)

    row = lax.broadcasted_iota(jnp.int32, (ny, nz), 0)
    lane = lax.broadcasted_iota(jnp.int32, (ny, nz), 1)

    def shifts(x, at_row=None, at_lane=None):
        first_row, last_row = (row == 0, row == ny - 1) if at_row is None else at_row
        first_lane, last_lane = (lane == 0, lane == nz - 1) if at_lane is None else at_lane
        return [
            jnp.where(first_row, 0.0, pltpu.roll(x, 1, 0)),
            jnp.where(last_row, 0.0, pltpu.roll(x, ny - 1, 0)),
            jnp.where(first_lane, 0.0, pltpu.roll(x, 1, 1)),
            jnp.where(last_lane, 0.0, pltpu.roll(x, nz - 1, 1)),
        ]

    def beside(x):
        up, down, left, right = shifts(x)
        return (up + down) + (left + right)

    clane = lax.broadcasted_iota(jnp.int32, (ncy, ncz), 1)

    def coarse_left(x):
        return jnp.where(clane == 0, 0.0, pltpu.roll(x, 1, 1))

    def coarse_right(x):
        return jnp.where(clane == ncz - 1, 0.0, pltpu.roll(x, ncz - 1, 1))

    def coarse_up(x):
        return pltpu.roll(x, 1, 0)

    def coarse_down(x):
        return pltpu.roll(x, ncy - 1, 0)

    def coarse_beside(x):
        return (coarse_up(x) + coarse_down(x)) + (coarse_left(x) + coarse_right(x))

    def coarsen(totals):
        pieces = [split(total) for total in totals]
        stacked = jnp.concatenate([p[0] for p in pieces] + [p[1] for p in pieces], axis=0).astype(BF16)
        product = jnp.dot(stacked, narrow[:, :ncz], preferred_element_type=F32)
        out = []
        for j in range(len(totals)):
            lower = (len(totals) + j) * ny
            slot = len(slots) % coarse_rows.shape[0]
            slots.append(slot)
            coarse_rows[slot, pl.ds(0, ny), :] = product[j * ny:(j + 1) * ny] + product[lower:lower + ny]
            parts = [coarse_rows[slot, pl.ds(k, ncy, stride=4), :] for k in range(4)]
            out.append(((parts[0] + parts[1]) + (parts[2] + parts[3])) * (1.0 / 64.0))
        return out

    slots = []

    with jax.named_scope("entry"):
        pl.semaphore_wait(
            barrier, 2 + 2 * sum(inside(d).astype(jnp.int32) for d in range(-REACH, REACH + 1) if d != 0)
        )

    send(starts.at[0, 0], p0.at[top], first[1], fine, -1, t)
    send(starts.at[0, last], p0.at[1], first[0], fine, 1, t)

    finish(load_sem, 5 * planes * fine)

    def coefficients(k):
        conduct = 1.0 / rho[k]
        mass = 1.0 + MASS_FLAG * moving[k].astype(F32)
        full = mass + 6.0 * STIFFNESS * conduct
        relax = RELAX / full
        stiff[k] = STIFFNESS * conduct
        diag[k] = full
        beta[k + 2] = (STIFFNESS * conduct) * relax
        for step in range(2):
            alpha[step, k] = (FORCE_WEIGHT * force[step, k]) * relax
        return mass, conduct

    def smooth(x, shift, i, below=True, above=True):
        here = x[i]
        around = beside(here)
        if below:
            around = around + x[i - 1]
        if above:
            around = around + x[i + 1]
        return here + (shift + beta[i] * (around - 6.0 * here))

    found = {0: coefficients(0)}
    send(beta.at[2, :, mine], beta.at[top, :, mine], first[1], fine // 2, -1, t)
    found[last] = coefficients(last)
    send(beta.at[last + 2, :, mine], beta.at[1, :, mine], first[0], fine // 2, 1, t)
    part_out[0] = smooth(p0, alpha[0, 0], 2, below=False)
    send(part_out.at[0], part_in.at[1], part[1], fine, -1, t)
    part_out[1] = smooth(p0, alpha[0, last], last + 2, above=False)
    send(part_out.at[1], part_in.at[0], part[0], fine, 1, t)
    for k in range(1, last):
        found[k] = coefficients(k)
        u0[k + 2] = smooth(p0, alpha[0, k], k + 2)

    mass_c = coarsen([functools.reduce(lambda a, b: a + b, [found[k][0] for k in range(planes)])])[0]
    conduct_c = coarsen([functools.reduce(lambda a, b: a + b, [found[k][1] for k in range(planes)])])[0]
    real = lax.broadcasted_iota(jnp.int32, (ncy, ncz), 0) < ny // 4
    relax_c = jnp.where(real, RELAX / jnp.where(real, mass_c + 6.0 * COARSE_STIFF * conduct_c, 1.0), 0.0)
    gam[REACH] = COARSE_STIFF * conduct_c * relax_c
    soft[2] = relax_c
    for d in order[:-2]:
        send(gam.at[REACH], gam.at[REACH - d], near[-d], coarse, d, t)
    send(soft.at[2], soft.at[1], near[1], coarse, -1, t)
    send(soft.at[2], soft.at[0], near[-1], coarse, 1, t)
    send(stiff.at[0, :, mine], hard.at[1, :, mine], stiffs[1], fine // 2, -1, t)
    send(stiff.at[last, :, mine], hard.at[0, :, mine], stiffs[0], fine // 2, 1, t)

    def block_sums(named):
        names = list(named)
        pieces = [split(named[name]) for name in names]
        stacked = jnp.concatenate([p[0] for p in pieces] + [p[1] for p in pieces], axis=0).astype(BF16)
        product = jnp.dot(stacked, narrow[...], preferred_element_type=F32)
        for j, name in enumerate(names):
            lower = (len(names) + j) * ny
            whole = product[j * ny:(j + 1) * ny] + product[lower:lower + ny]
            for cols in range(3):
                sums[SUMS.index(name), cols, pl.ds(0, ny), :] = whole[:, cols * ncz:(cols + 1) * ncz]

    with jax.named_scope("operator"):
        tile_rows = (row % 4 == 0, row % 4 == 3)
        tile_lanes = (lane % 4 == 0, lane % 4 == 3)
        total = {}
        for k in range(planes):
            stiff_k = stiff[k]
            up, down, left, right = shifts(stiff_k, tile_rows, tile_lanes)
            around = (up + down) + (left + right)
            if k > 0:
                around = around + stiff[k - 1]
            if k < last:
                around = around + stiff[k + 1]
            made = {"V": (1.0 - RELAX) * stiff_k + beta[k + 2] * around}
            for name, moved in zip(("ym", "yp", "zm", "zp"), shifts(beta[k + 2])):
                made[name] = stiff_k * moved
            for name, value in made.items():
                total[name] = total[name] + value if name in total else value
            if k in (0, last):
                block_sums({name + ("0" if k == 0 else "3"): value for name, value in made.items()})
        block_sums(total)

    def residual(prior, state, source):
        total = jnp.zeros((ny, nz), F32)
        for k in range(planes):
            here = state[k + 2]
            mass = 1.0 + MASS_FLAG * moving[k].astype(F32)
            around = beside(here)
            if k > 0:
                around = around + state[k + 1]
            if k < last:
                around = around + state[k + 3]
            total = total + (mass * prior[k + 2] + FORCE_WEIGHT * source[k]) - (diag[k] * here - stiff[k] * around)
        return total

    def pass_on(part, k, side):
        send(part, part, k, fine // 2, side, mate, to=me)

    for side, i in ((-1, 1), (1, top)):
        receive(first[side > 0], fine + fine // 2, side)
        pass_on(beta.at[i, :, mine], passed[side > 0], side)
    u0[2] = part_out[0] + beta[2] * p0[1]
    u0[last + 2] = part_out[1] + beta[last + 2] * p0[top]
    inner = residual(p0, u0, force.at[0])
    for side, i in ((-1, 1), (1, top)):
        receive(part[side > 0], fine, side)
        receive(passed[side > 0], fine // 2, side)
    u0[1] = part_in[0] + beta[1] * p0[2]
    u0[top] = part_in[1] + beta[top] * p0[last + 2]
    ring[0, REACH] = relax_c * coarsen([inner + (stiff[0] * u0[1] + stiff[last] * u0[top])])[0]
    for d in order:
        send(ring.at[0, REACH], ring.at[0, REACH - d], near[-d], coarse, d, t)

    b1[2] = smooth(u0, alpha[1, 0], 2)
    send(b1.at[2], b1.at[top], bases[1], fine, -1, t)
    b1[last + 2] = smooth(u0, alpha[1, last], last + 2)
    send(b1.at[last + 2], b1.at[1], bases[0], fine, 1, t)
    for side, i in ((-1, 0), (1, 1)):
        receive(stiffs[side > 0], fine // 2, side)
        pass_on(hard.at[i, :, mine], stiffs_passed[side > 0], side)
    for i in range(3, last + 2):
        b1[i] = smooth(u0, alpha[1, i - 2], i)
    inner = residual(u0, b1, force.at[1])
    block_sums({"xm": stiff[0] * beta[1], "xp": stiff[last] * beta[top]})

    def block_sum(name, rows=None, lanes="all"):
        j, cols = SUMS.index(name), {"all": 0, "zm": 1, "zp": 2}[lanes]
        if rows is not None:
            return sums[j, cols, pl.ds({"ym": 0, "yp": 3}[rows], ncy, stride=4), :]
        parts = [sums[j, cols, pl.ds(k, ncy, stride=4), :] for k in range(4)]
        return (parts[0] + parts[1]) + (parts[2] + parts[3])

    with jax.named_scope("points"):
        faces, edges = {}, {}
        for f in FACES:
            if f[0] == "x":
                faces[f] = block_sum("V0" if f == "xm" else "V3") - block_sum(f)
            elif f[0] == "y":
                faces[f] = block_sum("V", rows=f) - block_sum(f, rows=f)
            else:
                faces[f] = block_sum("V", lanes=f) - block_sum(f, lanes=f)
            for d in FACES:
                if d[0] == f[0]:
                    continue
                plane = f + {"xm": "0", "xp": "3"}.get(d, "")
                pick = {a[0]: a for a in (f, d)}
                edges[f, d] = block_sum(plane, rows=pick.get("y"), lanes=pick.get("z", "all"))
        scale = relax_c * (1.0 / 64.0)
        points = {"0": -functools.reduce(lambda a, b: a + b, faces.values())}
        for f in FACES:
            points[f] = faces[f] - functools.reduce(lambda a, b: a + b, [edges[f, d] for d in FACES if d[0] != f[0]])
        for f, d in EDGES:
            points[f + d] = edges[f, d] + edges[d, f]
        for j, name in enumerate(POINTS):
            operator[j] = scale * points[name]

    def corrected(errors):
        below, here, above = errors
        moves = {"ym": coarse_up, "yp": coarse_down, "zm": coarse_left, "zp": coarse_right}
        at = {"0": here, "xm": below, "xp": above}
        for f, move in moves.items():
            at[f] = move(here)
            for x in ("xm", "xp"):
                at[x + f] = move(at[x])
        for f in ("ym", "yp"):
            for d in ("zm", "zp"):
                at[f + d] = moves[f](at[d])
        terms = [operator[j] * at[name] for j, name in enumerate(POINTS)]
        while len(terms) > 1:
            terms = [a + b for a, b in zip(terms[::2], terms[1::2])] + ([terms[-1]] if len(terms) % 2 else [])
        return terms[0]

    plain = relax_c * coarsen([inner])[0]
    for d in order:
        receive(near[d], coarse * (3 if abs(d) == 1 else 2 if abs(d) < REACH else 1), d)

    def lend(state, step, tm, reach):
        below, above = coarsen([hard[0] * state[2], hard[1] * state[last + 2]])
        cross_out[step, 0] = soft[0] * below
        cross_out[step, 1] = soft[1] * above
        for d in range(-reach, reach + 1):
            if d == 0 and step == 1:
                cross[1, FAR] = cross_out[1]
            else:
                into = around_next if step == 0 else late
                send(cross_out.at[step], cross.at[step, FAR - d], into[-d], 2 * coarse, d, tm)

    def solve(step, width):
        right = {i: ring[step, i] for i in range(1 - width, SLOTS - 1 + width)}
        if step > 0:
            right = {i: x + (cross[step - 1, i, 1] + cross[step - 1, i + 2, 0]) for i, x in right.items()}
        error = right
        for sweep in range(COARSE_SWEEPS - 1):
            reach = COARSE_SWEEPS - 2 - sweep + width
            error = {
                i: (1.0 - RELAX) * error[i] + right[i]
                + gam[i] * (coarse_beside(error[i]) + (error[i - 1] + error[i + 1]))
                for i in range(REACH - reach, REACH + reach + 1)
            }
        return [error[i] for i in range(REACH - width, REACH + width + 1)]

    def expanded(errors):
        for j, error in enumerate(errors):
            for k in range(4):
                spread[j, pl.ds(k, ncy, stride=4), :] = error
        tall = jnp.concatenate([spread[j, pl.ds(0, ny), :] for j in range(len(errors))], axis=0)
        stacked = jnp.concatenate(split(tall), axis=1).astype(BF16)
        product = jnp.dot(stacked, wide[...], preferred_element_type=F32)
        return [product[j * ny:(j + 1) * ny] for j in range(len(errors))]

    errors = solve(0, 1)
    own[...] = plain + corrected(errors)
    for d in order + [0]:
        send(own, ring.at[1, REACH - d], around_next[-d], coarse, d, ahead)

    low, mid, high = expanded(errors)
    mid_change = beside(mid) - 4.0 * mid
    u1[2] = b1[2] + (mid + beta[2] * (mid_change + (low - mid)))
    for i in range(3, last + 2):
        u1[i] = b1[i] + (mid + beta[i] * mid_change)
    u1[last + 2] = b1[last + 2] + (mid + beta[last + 2] * (mid_change + (high - mid)))
    for side in (-1, 1):
        receive(bases[side > 0], fine, side)
    u1[1] = b1[1] + (low + beta[1] * (beside(low) - 4.0 * low + (mid - low)))
    u1[top] = b1[top] + (high + beta[top] * (beside(high) - 4.0 * high + (mid - high)))
    moved = pl.ds(1, planes + 2)
    send(u1.at[moved], came.at[moved], states, (planes + 2) * fine, 0, ahead)
    for side in (-1, 1):
        receive(stiffs_passed[side > 0], fine // 2, side)
    lend(b1, 0, ahead, FAR)
    receive(states, (planes + 2) * fine, 0)
    for i in range(2, top):
        v2[i] = smooth(came, alpha[0, i - 2], i)
    lend(v2, 1, t, REACH)
    plain = relax_c * coarsen([residual(came, v2, force.at[0])])[0]

    for d in range(-FAR, FAR + 1):
        receive(around_next[d], coarse * (3 if abs(d) < FAR else 2), d)
    errors = solve(1, 1)
    ring[2, REACH] = plain + corrected(errors)
    for d in order[:-2]:
        send(ring.at[2, REACH], ring.at[2, REACH - d], late[-d], coarse, d, t)

    low, mid, high = expanded(errors)
    change = beside(mid) - 4.0 * mid
    base_shift[...] = mid
    for k in range(planes):
        out_base[0, k] = came[k + 2]
        around = change + (low - mid) if k == 0 else change + (high - mid) if k == last else change
        out_state[0, k] = v2[k + 2] + (mid + beta[k + 2] * around)
    for d in order:
        receive(late[d], coarse * (3 if abs(d) < REACH else 2), d)
    state_shift[...] = expanded(solve(2, 0))[0]
    for d in range(-FAR, FAR + 1):
        when_inside(d, lambda d=d: finish(send_sem.at[d + FAR], sent[d]))


def solution(mesh):
    n, nt = mesh.shape["space"], mesh.shape["tm"]

    def local(slab_starts, forcing, density, moving_flags):
        _, planes, ny, nz = slab_starts.shape
        plane = (ny, nz)
        block = (planes,) + plane
        padded = (planes + 4,) + plane
        coarse = (8, nz // 4)
        result = jax.ShapeDtypeStruct(slab_starts.shape, F32)
        shift = jax.ShapeDtypeStruct(plane, F32)
        base, state, base_shift, state_shift = pl.pallas_call(
            functools.partial(kernel, n, nt, planes),
            out_shape=(result, result, shift, shift),
            in_specs=[pl.BlockSpec(memory_space=pl.ANY)] * 4,
            out_specs=(pl.BlockSpec(memory_space=pltpu.VMEM),) * 4,
            scratch_shapes=[
                pltpu.VMEM(padded, F32),
                pltpu.VMEM(padded, F32),
                pltpu.VMEM(padded, F32),
                pltpu.VMEM(padded, F32),
                pltpu.VMEM(padded, F32),
                pltpu.VMEM(padded, F32),
                pltpu.VMEM((2,) + block, F32),
                pltpu.VMEM(block, F32),
                pltpu.VMEM(block, jnp.int32),
                pltpu.VMEM(block, F32),
                pltpu.VMEM(block, F32),
                pltpu.VMEM((2,) + block, F32),
                pltpu.VMEM(padded, F32),
                pltpu.VMEM((2,) + plane, F32),
                pltpu.VMEM((2,) + plane, F32),
                pltpu.VMEM((2,) + plane, F32),
                pltpu.VMEM((3, SLOTS) + coarse, F32),
                pltpu.VMEM(coarse, F32),
                pltpu.VMEM((2, 2 * FAR + 1, 2) + coarse, F32),
                pltpu.VMEM((2, 2) + coarse, F32),
                pltpu.VMEM((SLOTS,) + coarse, F32),
                pltpu.VMEM((3,) + coarse, F32),
                pltpu.VMEM((4, 32, nz // 4), F32),
                pltpu.VMEM((len(SUMS), 3, 32, nz // 4), F32),
                pltpu.VMEM((len(POINTS),) + coarse, F32),
                pltpu.VMEM((2 * nz // 4, nz), BF16),
                pltpu.VMEM((nz, 3 * nz // 4), BF16),
                pltpu.VMEM((3, 32, nz // 4), F32),
                pltpu.VMEM((8 * planes * ny * nz // 128, 128), F32),
                pltpu.SemaphoreType.DMA,
                pltpu.SemaphoreType.DMA((2 * FAR + 1,)),
                pltpu.SemaphoreType.DMA((40,)),
            ],
            compiler_params=pltpu.CompilerParams(
                collective_id=0, has_side_effects=True, vmem_limit_bytes=32 * 1024 * 1024
            ),
            name="cycle",
        )(*[pltpu.with_memory_space_constraint(x, pltpu.HBM) for x in (slab_starts, forcing, density, moving_flags)])
        return base + base_shift, state + state_shift

    placed = (
        P("tm", "space", None, None),
        P("tm", None, "space", None, None),
        P("space", None, None),
        P("space", None, None),
    )
    return jax.shard_map(
        local,
        mesh=mesh,
        in_specs=placed,
        out_specs=(P("tm", "space", None, None), P("tm", "space", None, None)),
        check_vma=False,
    )
```

```python
import functools

import jax
import jax.numpy as jnp
from jax import lax
from jax.experimental import pallas as pl
from jax.experimental.pallas import tpu as pltpu
from jax.sharding import PartitionSpec as P

COARSE_SWEEPS = 4
STIFFNESS = 4.0
COARSE_STIFF = 0.25
FORCE_WEIGHT = 0.5
RELAX = 0.8
MASS_FLAG = 3.0

MESH = pl.DeviceIdType.MESH
REACH = COARSE_SWEEPS
SLOTS = 2 * REACH + 1
F32 = jnp.float32
BF16 = jnp.bfloat16

FACES = ("xm", "xp", "ym", "yp", "zm", "zp")
EDGES = [(f, d) for i, f in enumerate(FACES) for d in FACES[i + 1:] if f[0] != d[0]]
POINTS = ["0"] + list(FACES) + [f + d for f, d in EDGES]

OWN = ["V0", "V3", "V"] + [f + s for f in ("ym", "yp", "zm", "zp") for s in ("0", "3", "")]
BESIDE = ["xm", "xp"]
SUMS = OWN + BESIDE


def split(x):
    hi = x.astype(BF16).astype(F32)
    return [hi, (x - hi).astype(BF16).astype(F32)]


def kernel(
    n, nt, planes,
    starts, forcing, density, flags, out_base, out_state, base_shift, state_shift,
    p0, u0, b1, u1, came, v2, force, rho, moving, stiff, diag, alpha, beta, hard,
    part_in, part_out, ring, own, cross, gam, soft, coarse_rows, sums, operator, wide, narrow, spread, sizes,
    load_sem, gone_sem, send_sem, recv_sem,
):
    t = lax.axis_index("tm")
    me = lax.axis_index("space")
    ahead, behind = lax.rem(t + 1, nt), lax.rem(t + nt - 1, nt)
    half = lax.rem(t, 2)
    mate = t + 1 - 2 * half
    top = planes + 2
    last = planes - 1
    ny, nz = p0.shape[-2:]
    ncy, ncz = 8, nz // 4
    mine = pl.ds(pl.multiple_of(half * (nz // 2), nz // 2), nz // 2)
    theirs = pl.ds(pl.multiple_of((1 - half) * (nz // 2), nz // 2), nz // 2)

    def inside(offset):
        if offset < 0:
            return me >= -offset
        return me < n - offset

    order = [1, -1, 3, -3, 2, -2, 4, -4]

    barrier = pltpu.get_barrier_semaphore()
    for d in (1, -1, 2, -2, 3, -3, 4, -4):
        @pl.when(inside(d))
        def _(d=d):
            pl.semaphore_signal(barrier, inc=1, device_id=(t, me + d), device_id_type=MESH)
            pl.semaphore_signal(barrier, inc=1, device_id=(behind, me + d), device_id_type=MESH)
    pl.semaphore_signal(barrier, inc=1, device_id=(behind, me), device_id_type=MESH)
    pl.semaphore_signal(barrier, inc=1, device_id=(ahead, me), device_id_type=MESH)

    fine = ny * nz // 128
    coarse = ncy

    def finish(semaphore, rows):
        whole = sizes.at[pl.ds(0, rows)]
        pltpu.make_async_copy(whole, whole, semaphore).wait()

    for src, dst in (
        (density, rho), (flags, moving), (starts.at[0], p0.at[pl.ds(2, planes)]), (forcing.at[0], force),
    ):
        pltpu.make_async_copy(src, dst, load_sem).start()

    count = [jnp.minimum(me, REACH), jnp.minimum(n - 1 - me, REACH)]
    first, passed, part, further, hards, hards_passed, near, following, late = [[2 * j, 2 * j + 1] for j in range(9)]
    states = 18
    early, middle = 3, 2
    sent = {}

    def when_inside(offset, act):
        if offset == 0:
            act()
        else:
            pl.when(inside(offset))(act)

    def send(src, dst, k, rows, offset, tm, to=None, group=None):
        group = (int(offset > 0) if offset else middle) if group is None else group
        copy = pltpu.make_async_remote_copy(
            src_ref=src, dst_ref=dst, send_sem=send_sem.at[group], recv_sem=recv_sem.at[k],
            device_id=(tm, me + offset if to is None else to), device_id_type=MESH,
        )
        when_inside(offset, lambda: copy.start())
        rows_of = sent.setdefault(group, {})
        rows_of[abs(offset)] = rows_of.get(abs(offset), 0) + rows

    def finish_side(semaphore, side, rows_of):
        total = rows_of.get(0, 0)
        for distance in range(0, REACH + 1):
            if distance:
                total += rows_of.get(distance, 0)
            if total:
                pl.when(count[side] == distance)(lambda total=total: finish(semaphore, total))

    def receive(k, rows, offset):
        when_inside(offset, lambda: finish(recv_sem.at[k], rows))

    def receive_all(ks, rows_of):
        for side in range(2):
            finish_side(recv_sem.at[ks[side]], side, rows_of[side])

    for d in range(-REACH, REACH + 1):
        if d == 0:
            continue

        @pl.when(jnp.logical_not(inside(d)))
        def _(d=d):
            zero = jnp.zeros((ncy, ncz), F32)
            gam[REACH + d] = zero
            for step in range(3):
                ring[step, REACH + d] = zero
            for side in range(2):
                cross[REACH + d, side] = zero
            if abs(d) == 1:
                side = 0 if d < 0 else 1
                fine_zero = jnp.zeros((ny, nz), F32)
                edge = 1 if d < 0 else top
                p0[edge] = fine_zero
                beta[edge] = fine_zero
                hard[side] = fine_zero
                for step in range(2):
                    part_in[step, side] = fine_zero
                soft[side] = zero

    lane_of = lax.broadcasted_iota(jnp.int32, (nz, ncz), 0)
    block_of = lax.broadcasted_iota(jnp.int32, (nz, ncz), 1)
    for j, pick in enumerate([
        lane_of // 4 == block_of, lane_of == 4 * block_of, lane_of == 4 * block_of + 3,
    ]):
        narrow[:, j * ncz:(j + 1) * ncz] = pick.astype(F32).astype(BF16)
    one = (
        lax.broadcasted_iota(jnp.int32, (ncz, nz), 1) // 4 == lax.broadcasted_iota(jnp.int32, (ncz, nz), 0)
    ).astype(F32).astype(BF16)
    for piece in range(2):
        wide[pl.ds(piece * ncz, ncz), :] = one
    coarse_rows[...] = jnp.zeros_like(coarse_rows)
    for j in range(len(SUMS)):
        for cols in range(3):
            sums[j, cols, pl.ds(ny, 8), :] = jnp.zeros((8, ncz), F32)

    row = lax.broadcasted_iota(jnp.int32, (ny, nz), 0)
    lane = lax.broadcasted_iota(jnp.int32, (ny, nz), 1)

    def shifts(x, at_row=None, at_lane=None):
        first_row, last_row = (row == 0, row == ny - 1) if at_row is None else at_row
        first_lane, last_lane = (lane == 0, lane == nz - 1) if at_lane is None else at_lane
        return [
            jnp.where(first_row, 0.0, pltpu.roll(x, 1, 0)),
            jnp.where(last_row, 0.0, pltpu.roll(x, ny - 1, 0)),
            jnp.where(first_lane, 0.0, pltpu.roll(x, 1, 1)),
            jnp.where(last_lane, 0.0, pltpu.roll(x, nz - 1, 1)),
        ]

    def beside(x):
        up, down, left, right = shifts(x)
        return (up + down) + (left + right)

    clane = lax.broadcasted_iota(jnp.int32, (ncy, ncz), 1)

    def coarse_left(x):
        return jnp.where(clane == 0, 0.0, pltpu.roll(x, 1, 1))

    def coarse_right(x):
        return jnp.where(clane == ncz - 1, 0.0, pltpu.roll(x, ncz - 1, 1))

    def coarse_up(x):
        return pltpu.roll(x, 1, 0)

    def coarse_down(x):
        return pltpu.roll(x, ncy - 1, 0)

    def coarse_beside(x):
        return (coarse_up(x) + coarse_down(x)) + (coarse_left(x) + coarse_right(x))

    def coarsen(totals):
        pieces = [split(total) for total in totals]
        stacked = jnp.concatenate([p[0] for p in pieces] + [p[1] for p in pieces], axis=0).astype(BF16)
        product = jnp.dot(stacked, narrow[:, :ncz], preferred_element_type=F32)
        out = []
        for j in range(len(totals)):
            lower = (len(totals) + j) * ny
            slot = len(slots) % coarse_rows.shape[0]
            slots.append(slot)
            coarse_rows[slot, pl.ds(0, ny), :] = product[j * ny:(j + 1) * ny] + product[lower:lower + ny]
            parts = [coarse_rows[slot, pl.ds(k, ncy, stride=4), :] for k in range(4)]
            out.append(((parts[0] + parts[1]) + (parts[2] + parts[3])) * (1.0 / 64.0))
        return out

    slots = []

    with jax.named_scope("entry"):
        pl.semaphore_wait(
            barrier, 2 + 2 * sum(inside(d).astype(jnp.int32) for d in range(-REACH, REACH + 1) if d != 0)
        )

    send(starts.at[0, 0], p0.at[top], first[1], fine, -1, t, group=early)
    send(starts.at[0, last], p0.at[1], first[0], fine, 1, t, group=early + 1)

    finish(load_sem, 5 * planes * fine)

    def coefficients(k):
        conduct = 1.0 / rho[k]
        mass = 1.0 + MASS_FLAG * moving[k].astype(F32)
        full = mass + 6.0 * STIFFNESS * conduct
        relax = RELAX / full
        stiff[k] = STIFFNESS * conduct
        diag[k] = full
        beta[k + 2] = (STIFFNESS * conduct) * relax
        for step in range(2):
            alpha[step, k] = (FORCE_WEIGHT * force[step, k]) * relax
        return mass, conduct

    def smooth(x, shift, i, below=True, above=True):
        here = x[i]
        around = beside(here)
        if below:
            around = around + x[i - 1]
        if above:
            around = around + x[i + 1]
        return here + (shift + beta[i] * (around - 6.0 * here))

    found = {0: coefficients(0)}
    send(beta.at[2, :, mine], beta.at[top, :, mine], first[1], fine // 2, -1, t, group=early)
    found[last] = coefficients(last)
    send(beta.at[last + 2, :, mine], beta.at[1, :, mine], first[0], fine // 2, 1, t, group=early + 1)
    part_out[0, 0] = smooth(p0, alpha[0, 0], 2, below=False)
    send(part_out.at[0, 0], part_in.at[0, 1], part[1], fine, -1, t, group=early)
    part_out[0, 1] = smooth(p0, alpha[0, last], last + 2, above=False)
    send(part_out.at[0, 1], part_in.at[0, 0], part[0], fine, 1, t, group=early + 1)
    for k in range(1, last):
        found[k] = coefficients(k)
        u0[k + 2] = smooth(p0, alpha[0, k], k + 2)

    mass_c = coarsen([functools.reduce(lambda a, b: a + b, [found[k][0] for k in range(planes)])])[0]
    conduct_c = coarsen([functools.reduce(lambda a, b: a + b, [found[k][1] for k in range(planes)])])[0]
    real = lax.broadcasted_iota(jnp.int32, (ncy, ncz), 0) < ny // 4
    relax_c = jnp.where(real, RELAX / jnp.where(real, mass_c + 6.0 * COARSE_STIFF * conduct_c, 1.0), 0.0)
    gam[REACH] = COARSE_STIFF * conduct_c * relax_c
    soft[2] = relax_c
    for d in order[:-2]:
        send(gam.at[REACH], gam.at[REACH - d], near[d < 0], coarse, d, t)
    send(soft.at[2], soft.at[1], near[1], coarse, -1, t)
    send(soft.at[2], soft.at[0], near[0], coarse, 1, t)
    part_out[1, 0] = alpha[1, 0] + beta[2] * u0[3]
    part_out[1, 1] = alpha[1, last] + beta[last + 2] * u0[last + 1]

    def block_sums(named):
        names = list(named)
        pieces = [split(named[name]) for name in names]
        stacked = jnp.concatenate([p[0] for p in pieces] + [p[1] for p in pieces], axis=0).astype(BF16)
        product = jnp.dot(stacked, narrow[...], preferred_element_type=F32)
        for j, name in enumerate(names):
            lower = (len(names) + j) * ny
            whole = product[j * ny:(j + 1) * ny] + product[lower:lower + ny]
            for cols in range(3):
                sums[SUMS.index(name), cols, pl.ds(0, ny), :] = whole[:, cols * ncz:(cols + 1) * ncz]

    with jax.named_scope("operator"):
        tile_rows = (row % 4 == 0, row % 4 == 3)
        tile_lanes = (lane % 4 == 0, lane % 4 == 3)
        total = {}
        for k in range(planes):
            stiff_k = stiff[k]
            up, down, left, right = shifts(stiff_k, tile_rows, tile_lanes)
            around = (up + down) + (left + right)
            if k > 0:
                around = around + stiff[k - 1]
            if k < last:
                around = around + stiff[k + 1]
            made = {"V": (1.0 - RELAX) * stiff_k + beta[k + 2] * around}
            for name, moved in zip(("ym", "yp", "zm", "zp"), shifts(beta[k + 2])):
                made[name] = stiff_k * moved
            for name, value in made.items():
                total[name] = total[name] + value if name in total else value
            if k in (0, last):
                block_sums({name + ("0" if k == 0 else "3"): value for name, value in made.items()})
        block_sums(total)

    def residual(prior, state, source):
        total = jnp.zeros((ny, nz), F32)
        for k in range(planes):
            here = state[k + 2]
            mass = 1.0 + MASS_FLAG * moving[k].astype(F32)
            around = beside(here)
            if k > 0:
                around = around + state[k + 1]
            if k < last:
                around = around + state[k + 3]
            total = total + (mass * prior[k + 2] + FORCE_WEIGHT * source[k]) - (diag[k] * here - stiff[k] * around)
        return total

    def pass_on(part, k, side):
        send(part, part, k, fine // 2, side, mate, to=me)

    for side, i in ((-1, 1), (1, top)):
        receive(first[side > 0], fine + fine // 2, side)
        pass_on(beta.at[i, :, mine], passed[side > 0], side)
    u0[2] = part_out[0, 0] + beta[2] * p0[1]
    u0[last + 2] = part_out[0, 1] + beta[last + 2] * p0[top]
    inner = residual(p0, u0, force.at[0])
    for side in range(2):
        finish_side(send_sem.at[early + side], side, sent[early + side])
    pl.semaphore_signal(gone_sem, inc=1, device_id=(mate, me), device_id_type=MESH)
    pl.semaphore_wait(gone_sem, 1)
    send(part_out.at[1, 0], part_in.at[1, 1], further[1], fine, -1, t)
    send(part_out.at[1, 1], part_in.at[1, 0], further[0], fine, 1, t)
    for side, i in ((-1, 1), (1, top)):
        receive(part[side > 0], fine, side)
        receive(passed[side > 0], fine // 2, side)
    u0[1] = part_in[0, 0] + beta[1] * p0[2]
    u0[top] = part_in[0, 1] + beta[top] * p0[last + 2]
    ring[0, REACH] = relax_c * coarsen([inner + (stiff[0] * u0[1] + stiff[last] * u0[top])])[0]
    for d in order:
        send(ring.at[0, REACH], ring.at[0, REACH - d], near[d < 0], coarse, d, t)
    send(stiff.at[0, :, mine], hard.at[1, :, mine], hards[1], fine // 2, -1, t)
    send(stiff.at[last, :, mine], hard.at[0, :, mine], hards[0], fine // 2, 1, t)

    for i in range(2, top):
        b1[i] = smooth(u0, alpha[1, i - 2], i)
    inner = residual(u0, b1, force.at[1])
    block_sums({"xm": stiff[0] * beta[1], "xp": stiff[last] * beta[top]})

    def block_sum(name, rows=None, lanes="all"):
        j, cols = SUMS.index(name), {"all": 0, "zm": 1, "zp": 2}[lanes]
        if rows is not None:
            return sums[j, cols, pl.ds({"ym": 0, "yp": 3}[rows], ncy, stride=4), :]
        parts = [sums[j, cols, pl.ds(k, ncy, stride=4), :] for k in range(4)]
        return (parts[0] + parts[1]) + (parts[2] + parts[3])

    with jax.named_scope("points"):
        faces, edges = {}, {}
        for f in FACES:
            if f[0] == "x":
                faces[f] = block_sum("V0" if f == "xm" else "V3") - block_sum(f)
            elif f[0] == "y":
                faces[f] = block_sum("V", rows=f) - block_sum(f, rows=f)
            else:
                faces[f] = block_sum("V", lanes=f) - block_sum(f, lanes=f)
            for d in FACES:
                if d[0] == f[0]:
                    continue
                plane = f + {"xm": "0", "xp": "3"}.get(d, "")
                pick = {a[0]: a for a in (f, d)}
                edges[f, d] = block_sum(plane, rows=pick.get("y"), lanes=pick.get("z", "all"))
        scale = relax_c * (1.0 / 64.0)
        points = {"0": -functools.reduce(lambda a, b: a + b, faces.values())}
        for f in FACES:
            points[f] = faces[f] - functools.reduce(lambda a, b: a + b, [edges[f, d] for d in FACES if d[0] != f[0]])
        for f, d in EDGES:
            points[f + d] = edges[f, d] + edges[d, f]
        for j, name in enumerate(POINTS):
            operator[j] = scale * points[name]

    def corrected(errors):
        below, here, above = errors
        moves = {"ym": coarse_up, "yp": coarse_down, "zm": coarse_left, "zp": coarse_right}
        at = {"0": here, "xm": below, "xp": above}
        for f, move in moves.items():
            at[f] = move(here)
            for x in ("xm", "xp"):
                at[x + f] = move(at[x])
        for f in ("ym", "yp"):
            for d in ("zm", "zp"):
                at[f + d] = moves[f](at[d])
        terms = [operator[j] * at[name] for j, name in enumerate(POINTS)]
        while len(terms) > 1:
            terms = [a + b for a, b in zip(terms[::2], terms[1::2])] + ([terms[-1]] if len(terms) % 2 else [])
        return terms[0]

    for side, i, away in ((-1, 1, 0), (1, top, 1)):
        receive(further[side > 0], fine, side)
        b1[i] = smooth(u0, part_in[1, away], i, below=side > 0, above=side < 0)
    plain = relax_c * coarsen([inner + (stiff[0] * b1[1] + stiff[last] * b1[top])])[0]
    receive_all(near, [{d: coarse * (3 if d == 1 else 2 if d < REACH else 1) for d in range(1, REACH + 1)}] * 2)

    def solve(step, width):
        right = {i: ring[step, i] for i in range(1 - width, SLOTS - 1 + width)}
        if step == 2:
            right = {i: x + (cross[i - 1, 1] + cross[i + 1, 0]) for i, x in right.items()}
        error = right
        for sweep in range(COARSE_SWEEPS - 1):
            reach = COARSE_SWEEPS - 2 - sweep + width
            error = {
                i: (1.0 - RELAX) * error[i] + right[i]
                + gam[i] * (coarse_beside(error[i]) + (error[i - 1] + error[i + 1]))
                for i in range(REACH - reach, REACH + reach + 1)
            }
        return [error[i] for i in range(REACH - width, REACH + width + 1)]

    def expanded(errors):
        for j, error in enumerate(errors):
            for k in range(4):
                spread[j, pl.ds(k, ncy, stride=4), :] = error
        tall = jnp.concatenate([spread[j, pl.ds(0, ny), :] for j in range(len(errors))], axis=0)
        stacked = jnp.concatenate(split(tall), axis=1).astype(BF16)
        product = jnp.dot(stacked, wide[...], preferred_element_type=F32)
        return [product[j * ny:(j + 1) * ny] for j in range(len(errors))]

    errors = solve(0, 1)
    own[...] = plain + corrected(errors)
    for d in order + [0]:
        send(own, ring.at[1, REACH - d], following[d < 0], coarse, d, ahead)

    low, mid, high = expanded(errors)
    mid_change = beside(mid) - 4.0 * mid
    u1[2] = b1[2] + (mid + beta[2] * (mid_change + (low - mid)))
    for i in range(3, last + 2):
        u1[i] = b1[i] + (mid + beta[i] * mid_change)
    u1[last + 2] = b1[last + 2] + (mid + beta[last + 2] * (mid_change + (high - mid)))
    u1[1] = b1[1] + (low + beta[1] * (beside(low) - 4.0 * low + (mid - low)))
    u1[top] = b1[top] + (high + beta[top] * (beside(high) - 4.0 * high + (mid - high)))
    moved = pl.ds(1, planes + 2)
    send(u1.at[moved], came.at[moved], states, (planes + 2) * fine, 0, ahead)
    for side, i in ((-1, 0), (1, 1)):
        receive(hards[side > 0], fine // 2, side)
        pass_on(hard.at[i, :, mine], hards_passed[side > 0], side)
    receive(states, (planes + 2) * fine, 0)
    for i in range(2, top):
        v2[i] = smooth(came, alpha[0, i - 2], i)
    for side in (-1, 1):
        receive(hards_passed[side > 0], fine // 2, side)
    below, above = coarsen([hard[0] * v2[2], hard[1] * v2[last + 2]])
    cross[REACH, 0] = soft[0] * below
    cross[REACH, 1] = soft[1] * above
    for d in order:
        send(cross.at[REACH], cross.at[REACH - d], late[d < 0], 2 * coarse, d, t)
    plain = relax_c * coarsen([residual(came, v2, force.at[0])])[0]

    receive_all(following, [{d: coarse for d in range(low, REACH + 1)} for low in range(2)])
    errors = solve(1, 1)
    ring[2, REACH] = plain + corrected(errors)
    for d in order[:-2]:
        send(ring.at[2, REACH], ring.at[2, REACH - d], late[d < 0], coarse, d, t)

    low, mid, high = expanded(errors)
    change = beside(mid) - 4.0 * mid
    base_shift[...] = mid
    for k in range(planes):
        out_base[0, k] = came[k + 2]
        around = change + (low - mid) if k == 0 else change + (high - mid) if k == last else change
        out_state[0, k] = v2[k + 2] + (mid + beta[k + 2] * around)
    receive_all(late, [{d: coarse * (3 if d < REACH else 2) for d in range(1, REACH + 1)}] * 2)
    state_shift[...] = expanded(solve(2, 0))[0]
    for side in range(2):
        finish_side(send_sem.at[side], side, sent[side])
    finish(send_sem.at[middle], sent[middle][0])


def solution(mesh):
    n, nt = mesh.shape["space"], mesh.shape["tm"]

    def local(slab_starts, forcing, density, moving_flags):
        _, planes, ny, nz = slab_starts.shape
        plane = (ny, nz)
        block = (planes,) + plane
        padded = (planes + 4,) + plane
        coarse = (8, nz // 4)
        result = jax.ShapeDtypeStruct(slab_starts.shape, F32)
        shift = jax.ShapeDtypeStruct(plane, F32)
        base, state, base_shift, state_shift = pl.pallas_call(
            functools.partial(kernel, n, nt, planes),
            out_shape=(result, result, shift, shift),
            in_specs=[pl.BlockSpec(memory_space=pl.ANY)] * 4,
            out_specs=(pl.BlockSpec(memory_space=pltpu.VMEM),) * 4,
            scratch_shapes=[
                pltpu.VMEM(padded, F32),
                pltpu.VMEM(padded, F32),
                pltpu.VMEM(padded, F32),
                pltpu.VMEM(padded, F32),
                pltpu.VMEM(padded, F32),
                pltpu.VMEM(padded, F32),
                pltpu.VMEM((2,) + block, F32),
                pltpu.VMEM(block, F32),
                pltpu.VMEM(block, jnp.int32),
                pltpu.VMEM(block, F32),
                pltpu.VMEM(block, F32),
                pltpu.VMEM((2,) + block, F32),
                pltpu.VMEM(padded, F32),
                pltpu.VMEM((2,) + plane, F32),
                pltpu.VMEM((2, 2) + plane, F32),
                pltpu.VMEM((2, 2) + plane, F32),
                pltpu.VMEM((3, SLOTS) + coarse, F32),
                pltpu.VMEM(coarse, F32),
                pltpu.VMEM((SLOTS, 2) + coarse, F32),
                pltpu.VMEM((SLOTS,) + coarse, F32),
                pltpu.VMEM((3,) + coarse, F32),
                pltpu.VMEM((4, 32, nz // 4), F32),
                pltpu.VMEM((len(SUMS), 3, 32, nz // 4), F32),
                pltpu.VMEM((len(POINTS),) + coarse, F32),
                pltpu.VMEM((2 * nz // 4, nz), BF16),
                pltpu.VMEM((nz, 3 * nz // 4), BF16),
                pltpu.VMEM((3, 32, nz // 4), F32),
                pltpu.VMEM((8 * planes * ny * nz // 128, 128), F32),
                pltpu.SemaphoreType.DMA,
                pltpu.SemaphoreType.REGULAR,
                pltpu.SemaphoreType.DMA((5,)),
                pltpu.SemaphoreType.DMA((19,)),
            ],
            compiler_params=pltpu.CompilerParams(
                collective_id=0, has_side_effects=True, vmem_limit_bytes=32 * 1024 * 1024
            ),
            name="cycle",
        )(*[pltpu.with_memory_space_constraint(x, pltpu.HBM) for x in (slab_starts, forcing, density, moving_flags)])
        return base + base_shift, state + state_shift

    placed = (
        P("tm", "space", None, None),
        P("tm", None, "space", None, None),
        P("space", None, None),
        P("space", None, None),
    )
    return jax.shard_map(
        local,
        mesh=mesh,
        in_specs=placed,
        out_specs=(P("tm", "space", None, None), P("tm", "space", None, None)),
        check_vma=False,
    )
```

```python
import functools

import jax
import jax.numpy as jnp
from jax import lax
from jax.experimental import pallas as pl
from jax.experimental.pallas import tpu as pltpu
from jax.sharding import PartitionSpec as P

COARSE_SWEEPS = 4
STIFFNESS = 4.0
COARSE_STIFF = 0.25
FORCE_WEIGHT = 0.5
RELAX = 0.8
MASS_FLAG = 3.0

MESH = pl.DeviceIdType.MESH
REACH = COARSE_SWEEPS
SLOTS = 2 * REACH + 1
F32 = jnp.float32
BF16 = jnp.bfloat16

FACES = ("xm", "xp", "ym", "yp", "zm", "zp")
EDGES = [(f, d) for i, f in enumerate(FACES) for d in FACES[i + 1:] if f[0] != d[0]]
POINTS = ["0"] + list(FACES) + [f + d for f, d in EDGES]

OWN = ["V0", "V3", "V"] + [f + s for f in ("ym", "yp", "zm", "zp") for s in ("0", "3", "")]
BESIDE = ["xm", "xp"]
SUMS = OWN + BESIDE


def split(x):
    hi = x.astype(BF16).astype(F32)
    return [hi, (x - hi).astype(BF16).astype(F32)]


def kernel(
    n, nt, planes,
    starts, forcing, density, flags, out_base, out_state, base_shift, state_shift,
    p0, u0, b1, u1, came, v2, force, rho, moving, stiff, diag, alpha, beta, hard,
    part_in, part_out, ring, own, cross, gam, soft, coarse_rows, sums, operator, wide, narrow, spread, sizes,
    load_sem, gone_sem, send_sem, recv_sem,
):
    t = lax.axis_index("tm")
    me = lax.axis_index("space")
    ahead, behind = lax.rem(t + 1, nt), lax.rem(t + nt - 1, nt)
    half = lax.rem(t, 2)
    mate = t + 1 - 2 * half
    top = planes + 2
    last = planes - 1
    ny, nz = p0.shape[-2:]
    ncy, ncz = 8, nz // 4

    def inside(offset):
        if offset < 0:
            return me >= -offset
        return me < n - offset

    order = [1, -1, 3, -3, 2, -2, 4, -4]

    barrier = pltpu.get_barrier_semaphore()
    for d in (1, -1, 2, -2, 3, -3, 4, -4):
        @pl.when(inside(d))
        def _(d=d):
            pl.semaphore_signal(barrier, inc=1, device_id=(t, me + d), device_id_type=MESH)
            pl.semaphore_signal(barrier, inc=1, device_id=(behind, me + d), device_id_type=MESH)
    pl.semaphore_signal(barrier, inc=1, device_id=(behind, me), device_id_type=MESH)
    pl.semaphore_signal(barrier, inc=1, device_id=(ahead, me), device_id_type=MESH)

    fine = ny * nz // 128
    coarse = ncy

    def finish(semaphore, rows):
        whole = sizes.at[pl.ds(0, rows)]
        pltpu.make_async_copy(whole, whole, semaphore).wait()

    for src, dst in (
        (density, rho), (flags, moving), (starts.at[0], p0.at[pl.ds(2, planes)]), (forcing.at[0], force),
    ):
        pltpu.make_async_copy(src, dst, load_sem).start()

    count = [jnp.minimum(me, REACH), jnp.minimum(n - 1 - me, REACH)]
    first, betas, passed, part, further, hards, hards_passed, near, following, late = [
        [2 * j, 2 * j + 1] for j in range(10)
    ]
    states = 20
    early, second, coefs, told, middle = 3, 5, 7, 9, 2
    teller = half == 1
    sent = {}

    def when_inside(offset, act, only=None):
        if offset == 0:
            act()
        else:
            pl.when(inside(offset) if only is None else jnp.logical_and(only, inside(offset)))(act)

    def send(src, dst, k, rows, offset, tm, to=None, group=None, only=None):
        group = (int(offset > 0) if offset else middle) if group is None else group
        copy = pltpu.make_async_remote_copy(
            src_ref=src, dst_ref=dst, send_sem=send_sem.at[group], recv_sem=recv_sem.at[k],
            device_id=(tm, me + offset if to is None else to), device_id_type=MESH,
        )
        when_inside(offset, lambda: copy.start(), only)
        rows_of = sent.setdefault(group, {})
        rows_of[abs(offset)] = rows_of.get(abs(offset), 0) + rows

    def finish_side(semaphore, side, rows_of):
        total = rows_of.get(0, 0)
        for distance in range(0, REACH + 1):
            if distance:
                total += rows_of.get(distance, 0)
            if total:
                pl.when(count[side] == distance)(lambda total=total: finish(semaphore, total))

    def receive(k, rows, offset, only=None):
        when_inside(offset, lambda: finish(recv_sem.at[k], rows), only)

    def receive_all(ks, rows_of):
        for side in range(2):
            finish_side(recv_sem.at[ks[side]], side, rows_of[side])

    for d in range(-REACH, REACH + 1):
        if d == 0:
            continue

        @pl.when(jnp.logical_not(inside(d)))
        def _(d=d):
            zero = jnp.zeros((ncy, ncz), F32)
            gam[REACH + d] = zero
            for step in range(3):
                ring[step, REACH + d] = zero
            for side in range(2):
                cross[REACH + d, side] = zero
            if abs(d) == 1:
                side = 0 if d < 0 else 1
                fine_zero = jnp.zeros((ny, nz), F32)
                edge = 1 if d < 0 else top
                p0[edge] = fine_zero
                beta[edge] = fine_zero
                hard[side] = fine_zero
                for step in range(2):
                    part_in[step, side] = fine_zero
                soft[side] = zero

    lane_of = lax.broadcasted_iota(jnp.int32, (nz, ncz), 0)
    block_of = lax.broadcasted_iota(jnp.int32, (nz, ncz), 1)
    for j, pick in enumerate([
        lane_of // 4 == block_of, lane_of == 4 * block_of, lane_of == 4 * block_of + 3,
    ]):
        narrow[:, j * ncz:(j + 1) * ncz] = pick.astype(F32).astype(BF16)
    one = (
        lax.broadcasted_iota(jnp.int32, (ncz, nz), 1) // 4 == lax.broadcasted_iota(jnp.int32, (ncz, nz), 0)
    ).astype(F32).astype(BF16)
    for piece in range(2):
        wide[pl.ds(piece * ncz, ncz), :] = one
    coarse_rows[...] = jnp.zeros_like(coarse_rows)
    for j in range(len(SUMS)):
        for cols in range(3):
            sums[j, cols, pl.ds(ny, 8), :] = jnp.zeros((8, ncz), F32)

    row = lax.broadcasted_iota(jnp.int32, (ny, nz), 0)
    lane = lax.broadcasted_iota(jnp.int32, (ny, nz), 1)

    def shifts(x, at_row=None, at_lane=None):
        first_row, last_row = (row == 0, row == ny - 1) if at_row is None else at_row
        first_lane, last_lane = (lane == 0, lane == nz - 1) if at_lane is None else at_lane
        return [
            jnp.where(first_row, 0.0, pltpu.roll(x, 1, 0)),
            jnp.where(last_row, 0.0, pltpu.roll(x, ny - 1, 0)),
            jnp.where(first_lane, 0.0, pltpu.roll(x, 1, 1)),
            jnp.where(last_lane, 0.0, pltpu.roll(x, nz - 1, 1)),
        ]

    def beside(x):
        up, down, left, right = shifts(x)
        return (up + down) + (left + right)

    clane = lax.broadcasted_iota(jnp.int32, (ncy, ncz), 1)

    def coarse_left(x):
        return jnp.where(clane == 0, 0.0, pltpu.roll(x, 1, 1))

    def coarse_right(x):
        return jnp.where(clane == ncz - 1, 0.0, pltpu.roll(x, ncz - 1, 1))

    def coarse_up(x):
        return pltpu.roll(x, 1, 0)

    def coarse_down(x):
        return pltpu.roll(x, ncy - 1, 0)

    def coarse_beside(x):
        return (coarse_up(x) + coarse_down(x)) + (coarse_left(x) + coarse_right(x))

    def coarsen(totals):
        pieces = [split(total) for total in totals]
        stacked = jnp.concatenate([p[0] for p in pieces] + [p[1] for p in pieces], axis=0).astype(BF16)
        product = jnp.dot(stacked, narrow[:, :ncz], preferred_element_type=F32)
        out = []
        for j in range(len(totals)):
            lower = (len(totals) + j) * ny
            slot = len(slots) % coarse_rows.shape[0]
            slots.append(slot)
            coarse_rows[slot, pl.ds(0, ny), :] = product[j * ny:(j + 1) * ny] + product[lower:lower + ny]
            parts = [coarse_rows[slot, pl.ds(k, ncy, stride=4), :] for k in range(4)]
            out.append(((parts[0] + parts[1]) + (parts[2] + parts[3])) * (1.0 / 64.0))
        return out

    slots = []

    with jax.named_scope("entry"):
        pl.semaphore_wait(
            barrier, 2 + 2 * sum(inside(d).astype(jnp.int32) for d in range(-REACH, REACH + 1) if d != 0)
        )

    send(starts.at[0, 0], p0.at[top], first[1], fine, -1, t, group=early)
    send(starts.at[0, last], p0.at[1], first[0], fine, 1, t, group=early + 1)

    finish(load_sem, 5 * planes * fine)

    def coefficients(k):
        conduct = 1.0 / rho[k]
        mass = 1.0 + MASS_FLAG * moving[k].astype(F32)
        full = mass + 6.0 * STIFFNESS * conduct
        relax = RELAX / full
        stiff[k] = STIFFNESS * conduct
        diag[k] = full
        beta[k + 2] = (STIFFNESS * conduct) * relax
        for step in range(2):
            alpha[step, k] = (FORCE_WEIGHT * force[step, k]) * relax
        return mass, conduct

    def smooth(x, shift, i, below=True, above=True):
        here = x[i]
        around = beside(here)
        if below:
            around = around + x[i - 1]
        if above:
            around = around + x[i + 1]
        return here + (shift + beta[i] * (around - 6.0 * here))

    found = {0: coefficients(0)}
    send(beta.at[2], beta.at[top], betas[1], fine, -1, t, group=coefs, only=teller)
    found[last] = coefficients(last)
    send(beta.at[last + 2], beta.at[1], betas[0], fine, 1, t, group=coefs + 1, only=teller)
    part_out[0, 0] = smooth(p0, alpha[0, 0], 2, below=False)
    send(part_out.at[0, 0], part_in.at[0, 1], part[1], fine, -1, t, group=early)
    part_out[0, 1] = smooth(p0, alpha[0, last], last + 2, above=False)
    send(part_out.at[0, 1], part_in.at[0, 0], part[0], fine, 1, t, group=early + 1)
    for k in range(1, last):
        found[k] = coefficients(k)
        u0[k + 2] = smooth(p0, alpha[0, k], k + 2)

    mass_c = coarsen([functools.reduce(lambda a, b: a + b, [found[k][0] for k in range(planes)])])[0]
    conduct_c = coarsen([functools.reduce(lambda a, b: a + b, [found[k][1] for k in range(planes)])])[0]
    real = lax.broadcasted_iota(jnp.int32, (ncy, ncz), 0) < ny // 4
    relax_c = jnp.where(real, RELAX / jnp.where(real, mass_c + 6.0 * COARSE_STIFF * conduct_c, 1.0), 0.0)
    gam[REACH] = COARSE_STIFF * conduct_c * relax_c
    soft[2] = relax_c
    for d in order[:-2]:
        send(gam.at[REACH], gam.at[REACH - d], near[d < 0], coarse, d, t)
    send(soft.at[2], soft.at[1], near[1], coarse, -1, t)
    send(soft.at[2], soft.at[0], near[0], coarse, 1, t)
    part_out[1, 0] = alpha[1, 0] + beta[2] * u0[3]
    part_out[1, 1] = alpha[1, last] + beta[last + 2] * u0[last + 1]

    def block_sums(named):
        names = list(named)
        pieces = [split(named[name]) for name in names]
        stacked = jnp.concatenate([p[0] for p in pieces] + [p[1] for p in pieces], axis=0).astype(BF16)
        product = jnp.dot(stacked, narrow[...], preferred_element_type=F32)
        for j, name in enumerate(names):
            lower = (len(names) + j) * ny
            whole = product[j * ny:(j + 1) * ny] + product[lower:lower + ny]
            for cols in range(3):
                sums[SUMS.index(name), cols, pl.ds(0, ny), :] = whole[:, cols * ncz:(cols + 1) * ncz]

    with jax.named_scope("operator"):
        tile_rows = (row % 4 == 0, row % 4 == 3)
        tile_lanes = (lane % 4 == 0, lane % 4 == 3)
        total = {}
        for k in range(planes):
            stiff_k = stiff[k]
            up, down, left, right = shifts(stiff_k, tile_rows, tile_lanes)
            around = (up + down) + (left + right)
            if k > 0:
                around = around + stiff[k - 1]
            if k < last:
                around = around + stiff[k + 1]
            made = {"V": (1.0 - RELAX) * stiff_k + beta[k + 2] * around}
            for name, moved in zip(("ym", "yp", "zm", "zp"), shifts(beta[k + 2])):
                made[name] = stiff_k * moved
            for name, value in made.items():
                total[name] = total[name] + value if name in total else value
            if k in (0, last):
                block_sums({name + ("0" if k == 0 else "3"): value for name, value in made.items()})
        block_sums(total)

    def residual(prior, state, source):
        total = jnp.zeros((ny, nz), F32)
        for k in range(planes):
            here = state[k + 2]
            mass = 1.0 + MASS_FLAG * moving[k].astype(F32)
            around = beside(here)
            if k > 0:
                around = around + state[k + 1]
            if k < last:
                around = around + state[k + 3]
            total = total + (mass * prior[k + 2] + FORCE_WEIGHT * source[k]) - (diag[k] * here - stiff[k] * around)
        return total

    def pass_on(part, k, side):
        send(part, part, k, fine, side, mate, to=me, group=told + (side > 0), only=teller)

    soon = functools.reduce(jnp.logical_or, [lax.rem(me, 4) == k for k in (1, 2)])

    def send_further(condition):
        @pl.when(condition)
        def _():
            for side in range(2):
                finish_side(send_sem.at[early + side], side, sent[early + side])
            pl.semaphore_signal(gone_sem, inc=1, device_id=(mate, me), device_id_type=MESH)
            pl.semaphore_wait(gone_sem, 1)
            send(part_out.at[1, 0], part_in.at[1, 1], further[1], fine, -1, t, group=second)
            send(part_out.at[1, 1], part_in.at[1, 0], further[0], fine, 1, t, group=second + 1)

    send_further(soon)

    for side, i in ((-1, 1), (1, top)):
        receive(first[side > 0], fine, side)
        receive(betas[side > 0], fine, side, only=teller)
        pass_on(beta.at[i], passed[side > 0], side)
    u0[2] = part_out[0, 0] + beta[2] * p0[1]
    u0[last + 2] = part_out[0, 1] + beta[last + 2] * p0[top]
    inner = residual(p0, u0, force.at[0])
    send_further(jnp.logical_not(soon))
    for side, i in ((-1, 1), (1, top)):
        receive(part[side > 0], fine, side)
        receive(passed[side > 0], fine, side, only=jnp.logical_not(teller))
    u0[1] = part_in[0, 0] + beta[1] * p0[2]
    u0[top] = part_in[0, 1] + beta[top] * p0[last + 2]
    ring[0, REACH] = relax_c * coarsen([inner + (stiff[0] * u0[1] + stiff[last] * u0[top])])[0]
    for d in order:
        send(ring.at[0, REACH], ring.at[0, REACH - d], near[d < 0], coarse, d, t)

    for i in range(2, top):
        b1[i] = smooth(u0, alpha[1, i - 2], i)
    inner = residual(u0, b1, force.at[1])
    block_sums({"xm": stiff[0] * beta[1], "xp": stiff[last] * beta[top]})

    def block_sum(name, rows=None, lanes="all"):
        j, cols = SUMS.index(name), {"all": 0, "zm": 1, "zp": 2}[lanes]
        if rows is not None:
            return sums[j, cols, pl.ds({"ym": 0, "yp": 3}[rows], ncy, stride=4), :]
        parts = [sums[j, cols, pl.ds(k, ncy, stride=4), :] for k in range(4)]
        return (parts[0] + parts[1]) + (parts[2] + parts[3])

    with jax.named_scope("points"):
        faces, edges = {}, {}
        for f in FACES:
            if f[0] == "x":
                faces[f] = block_sum("V0" if f == "xm" else "V3") - block_sum(f)
            elif f[0] == "y":
                faces[f] = block_sum("V", rows=f) - block_sum(f, rows=f)
            else:
                faces[f] = block_sum("V", lanes=f) - block_sum(f, lanes=f)
            for d in FACES:
                if d[0] == f[0]:
                    continue
                plane = f + {"xm": "0", "xp": "3"}.get(d, "")
                pick = {a[0]: a for a in (f, d)}
                edges[f, d] = block_sum(plane, rows=pick.get("y"), lanes=pick.get("z", "all"))
        scale = relax_c * (1.0 / 64.0)
        points = {"0": -functools.reduce(lambda a, b: a + b, faces.values())}
        for f in FACES:
            points[f] = faces[f] - functools.reduce(lambda a, b: a + b, [edges[f, d] for d in FACES if d[0] != f[0]])
        for f, d in EDGES:
            points[f + d] = edges[f, d] + edges[d, f]
        for j, name in enumerate(POINTS):
            operator[j] = scale * points[name]

    def corrected(errors):
        below, here, above = errors
        moves = {"ym": coarse_up, "yp": coarse_down, "zm": coarse_left, "zp": coarse_right}
        at = {"0": here, "xm": below, "xp": above}
        for f, move in moves.items():
            at[f] = move(here)
            for x in ("xm", "xp"):
                at[x + f] = move(at[x])
        for f in ("ym", "yp"):
            for d in ("zm", "zp"):
                at[f + d] = moves[f](at[d])
        terms = [operator[j] * at[name] for j, name in enumerate(POINTS)]
        while len(terms) > 1:
            terms = [a + b for a, b in zip(terms[::2], terms[1::2])] + ([terms[-1]] if len(terms) % 2 else [])
        return terms[0]

    for side in range(2):
        finish_side(send_sem.at[second + side], side, {1: fine})
    send(stiff.at[0], hard.at[1], hards[1], fine, -1, t, group=coefs, only=teller)
    send(stiff.at[last], hard.at[0], hards[0], fine, 1, t, group=coefs + 1, only=teller)
    for side, i, away in ((-1, 1, 0), (1, top, 1)):
        receive(further[side > 0], fine, side)
        b1[i] = smooth(u0, part_in[1, away], i, below=side > 0, above=side < 0)
    plain = relax_c * coarsen([inner + (stiff[0] * b1[1] + stiff[last] * b1[top])])[0]
    receive_all(near, [{d: coarse * (3 if d == 1 else 2 if d < REACH else 1) for d in range(1, REACH + 1)}] * 2)

    def solve(step, width):
        right = {i: ring[step, i] for i in range(1 - width, SLOTS - 1 + width)}
        if step == 2:
            right = {i: x + (cross[i - 1, 1] + cross[i + 1, 0]) for i, x in right.items()}
        error = right
        for sweep in range(COARSE_SWEEPS - 1):
            reach = COARSE_SWEEPS - 2 - sweep + width
            error = {
                i: (1.0 - RELAX) * error[i] + right[i]
                + gam[i] * (coarse_beside(error[i]) + (error[i - 1] + error[i + 1]))
                for i in range(REACH - reach, REACH + reach + 1)
            }
        return [error[i] for i in range(REACH - width, REACH + width + 1)]

    def expanded(errors):
        for j, error in enumerate(errors):
            for k in range(4):
                spread[j, pl.ds(k, ncy, stride=4), :] = error
        tall = jnp.concatenate([spread[j, pl.ds(0, ny), :] for j in range(len(errors))], axis=0)
        stacked = jnp.concatenate(split(tall), axis=1).astype(BF16)
        product = jnp.dot(stacked, wide[...], preferred_element_type=F32)
        return [product[j * ny:(j + 1) * ny] for j in range(len(errors))]

    errors = solve(0, 1)
    own[...] = plain + corrected(errors)
    for d in order + [0]:
        send(own, ring.at[1, REACH - d], following[d < 0], coarse, d, ahead)

    low, mid, high = expanded(errors)
    mid_change = beside(mid) - 4.0 * mid
    u1[2] = b1[2] + (mid + beta[2] * (mid_change + (low - mid)))
    for i in range(3, last + 2):
        u1[i] = b1[i] + (mid + beta[i] * mid_change)
    u1[last + 2] = b1[last + 2] + (mid + beta[last + 2] * (mid_change + (high - mid)))
    u1[1] = b1[1] + (low + beta[1] * (beside(low) - 4.0 * low + (mid - low)))
    u1[top] = b1[top] + (high + beta[top] * (beside(high) - 4.0 * high + (mid - high)))
    moved = pl.ds(1, planes + 2)
    send(u1.at[moved], came.at[moved], states, (planes + 2) * fine, 0, ahead)
    for side, i in ((-1, 0), (1, 1)):
        receive(hards[side > 0], fine, side, only=teller)
        pass_on(hard.at[i], hards_passed[side > 0], side)
    receive(states, (planes + 2) * fine, 0)
    for i in range(2, top):
        v2[i] = smooth(came, alpha[0, i - 2], i)
    for side in (-1, 1):
        receive(hards_passed[side > 0], fine, side, only=jnp.logical_not(teller))
    below, above = coarsen([hard[0] * v2[2], hard[1] * v2[last + 2]])
    cross[REACH, 0] = soft[0] * below
    cross[REACH, 1] = soft[1] * above
    for d in order:
        send(cross.at[REACH], cross.at[REACH - d], late[d < 0], 2 * coarse, d, t)
    plain = relax_c * coarsen([residual(came, v2, force.at[0])])[0]

    receive_all(following, [{d: coarse for d in range(low, REACH + 1)} for low in range(2)])
    errors = solve(1, 1)
    ring[2, REACH] = plain + corrected(errors)
    for d in order[:-2]:
        send(ring.at[2, REACH], ring.at[2, REACH - d], late[d < 0], coarse, d, t)

    low, mid, high = expanded(errors)
    change = beside(mid) - 4.0 * mid
    base_shift[...] = mid
    for k in range(planes):
        out_base[0, k] = came[k + 2]
        around = change + (low - mid) if k == 0 else change + (high - mid) if k == last else change
        out_state[0, k] = v2[k + 2] + (mid + beta[k + 2] * around)
    receive_all(late, [{d: coarse * (3 if d < REACH else 2) for d in range(1, REACH + 1)}] * 2)
    state_shift[...] = expanded(solve(2, 0))[0]
    for side in range(2):
        finish_side(send_sem.at[side], side, sent[side])
        for group in (coefs, told):
            when_inside(2 * side - 1, lambda side=side, group=group: finish(send_sem.at[group + side], 2 * fine), teller)
    finish(send_sem.at[middle], sent[middle][0])


def solution(mesh):
    n, nt = mesh.shape["space"], mesh.shape["tm"]

    def local(slab_starts, forcing, density, moving_flags):
        _, planes, ny, nz = slab_starts.shape
        plane = (ny, nz)
        block = (planes,) + plane
        padded = (planes + 4,) + plane
        coarse = (8, nz // 4)
        result = jax.ShapeDtypeStruct(slab_starts.shape, F32)
        shift = jax.ShapeDtypeStruct(plane, F32)
        base, state, base_shift, state_shift = pl.pallas_call(
            functools.partial(kernel, n, nt, planes),
            out_shape=(result, result, shift, shift),
            in_specs=[pl.BlockSpec(memory_space=pl.ANY)] * 4,
            out_specs=(pl.BlockSpec(memory_space=pltpu.VMEM),) * 4,
            scratch_shapes=[
                pltpu.VMEM(padded, F32),
                pltpu.VMEM(padded, F32),
                pltpu.VMEM(padded, F32),
                pltpu.VMEM(padded, F32),
                pltpu.VMEM(padded, F32),
                pltpu.VMEM(padded, F32),
                pltpu.VMEM((2,) + block, F32),
                pltpu.VMEM(block, F32),
                pltpu.VMEM(block, jnp.int32),
                pltpu.VMEM(block, F32),
                pltpu.VMEM(block, F32),
                pltpu.VMEM((2,) + block, F32),
                pltpu.VMEM(padded, F32),
                pltpu.VMEM((2,) + plane, F32),
                pltpu.VMEM((2, 2) + plane, F32),
                pltpu.VMEM((2, 2) + plane, F32),
                pltpu.VMEM((3, SLOTS) + coarse, F32),
                pltpu.VMEM(coarse, F32),
                pltpu.VMEM((SLOTS, 2) + coarse, F32),
                pltpu.VMEM((SLOTS,) + coarse, F32),
                pltpu.VMEM((3,) + coarse, F32),
                pltpu.VMEM((4, 32, nz // 4), F32),
                pltpu.VMEM((len(SUMS), 3, 32, nz // 4), F32),
                pltpu.VMEM((len(POINTS),) + coarse, F32),
                pltpu.VMEM((2 * nz // 4, nz), BF16),
                pltpu.VMEM((nz, 3 * nz // 4), BF16),
                pltpu.VMEM((3, 32, nz // 4), F32),
                pltpu.VMEM((8 * planes * ny * nz // 128, 128), F32),
                pltpu.SemaphoreType.DMA,
                pltpu.SemaphoreType.REGULAR,
                pltpu.SemaphoreType.DMA((11,)),
                pltpu.SemaphoreType.DMA((21,)),
            ],
            compiler_params=pltpu.CompilerParams(
                collective_id=0, has_side_effects=True, vmem_limit_bytes=32 * 1024 * 1024
            ),
            name="cycle",
        )(*[pltpu.with_memory_space_constraint(x, pltpu.HBM) for x in (slab_starts, forcing, density, moving_flags)])
        return base + base_shift, state + state_shift

    placed = (
        P("tm", "space", None, None),
        P("tm", None, "space", None, None),
        P("space", None, None),
        P("space", None, None),
    )
    return jax.shard_map(
        local,
        mesh=mesh,
        in_specs=placed,
        out_specs=(P("tm", "space", None, None), P("tm", "space", None, None)),
        check_vma=False,
    )
```

```python
import functools

import jax
import jax.numpy as jnp
from jax import lax
from jax.experimental import pallas as pl
from jax.experimental.pallas import tpu as pltpu
from jax.sharding import PartitionSpec as P

COARSE_SWEEPS = 4
STIFFNESS = 4.0
COARSE_STIFF = 0.25
FORCE_WEIGHT = 0.5
RELAX = 0.8
MASS_FLAG = 3.0

MESH = pl.DeviceIdType.MESH
REACH = COARSE_SWEEPS
SLOTS = 2 * REACH + 1
F32 = jnp.float32
BF16 = jnp.bfloat16

FACES = ("xm", "xp", "ym", "yp", "zm", "zp")
EDGES = [(f, d) for i, f in enumerate(FACES) for d in FACES[i + 1:] if f[0] != d[0]]
POINTS = ["0"] + list(FACES) + [f + d for f, d in EDGES]

OWN = ["V0", "V3", "V"] + [f + s for f in ("ym", "yp", "zm", "zp") for s in ("0", "3", "")]
BESIDE = ["xm", "xp"]
SUMS = OWN + BESIDE


def split(x):
    hi = x.astype(BF16).astype(F32)
    return [hi, (x - hi).astype(BF16).astype(F32)]


def kernel(
    n, nt, planes,
    starts, forcing, density, flags, out_base, out_state, base_shift, state_shift,
    p0, u0, b1, u1, came, v2, force, rho, moving, stiff, diag, alpha, beta, hard,
    part_in, part_out, ring, own, cross, gam, soft, coarse_rows, sums, operator, wide, narrow, spread, sizes,
    load_sem, gone_sem, known_sem, send_sem, recv_sem,
):
    t = lax.axis_index("tm")
    me = lax.axis_index("space")
    ahead, behind = lax.rem(t + 1, nt), lax.rem(t + nt - 1, nt)
    half = lax.rem(t, 2)
    mate = t + 1 - 2 * half
    top = planes + 2
    last = planes - 1
    ny, nz = p0.shape[-2:]
    ncy, ncz = 8, nz // 4

    def inside(offset):
        if offset < 0:
            return me >= -offset
        return me < n - offset

    order = [1, -1, 3, -3, 2, -2, 4, -4]

    barrier = pltpu.get_barrier_semaphore()
    neighbours = inside(-1).astype(jnp.int32) + inside(1).astype(jnp.int32)

    def tell(semaphore):
        for d in (1, -1):
            @pl.when(inside(d))
            def _(d=d):
                pl.semaphore_signal(semaphore, inc=1, device_id=(t, me + d), device_id_type=MESH)

    tell(barrier)
    pl.semaphore_signal(barrier, inc=1, device_id=(behind, me), device_id_type=MESH)
    pl.semaphore_signal(barrier, inc=1, device_id=(ahead, me), device_id_type=MESH)

    fine = ny * nz // 128
    coarse = ncy

    def finish(semaphore, rows):
        whole = sizes.at[pl.ds(0, rows)]
        pltpu.make_async_copy(whole, whole, semaphore).wait()

    for src, dst in (
        (density, rho), (flags, moving), (starts.at[0], p0.at[pl.ds(2, planes)]), (forcing.at[0], force),
    ):
        pltpu.make_async_copy(src, dst, load_sem).start()

    count = [jnp.minimum(me, REACH), jnp.minimum(n - 1 - me, REACH)]
    first, betas, passed, part, further, hards, hards_passed, near, following, late = [
        [2 * j, 2 * j + 1] for j in range(10)
    ]
    states = 20
    early, second, coefs, told, middle = 3, 5, 7, 9, 2
    teller = half == 1
    other = half == 0
    sent = {}

    def when_inside(offset, act, only=None):
        if offset == 0:
            act()
        else:
            pl.when(inside(offset) if only is None else jnp.logical_and(only, inside(offset)))(act)

    def send(src, dst, k, rows, offset, tm, to=None, group=None, only=None):
        group = (int(offset > 0) if offset else middle) if group is None else group
        copy = pltpu.make_async_remote_copy(
            src_ref=src, dst_ref=dst, send_sem=send_sem.at[group], recv_sem=recv_sem.at[k],
            device_id=(tm, me + offset if to is None else to), device_id_type=MESH,
        )
        when_inside(offset, lambda: copy.start(), only)
        rows_of = sent.setdefault(group, {})
        rows_of[abs(offset)] = rows_of.get(abs(offset), 0) + rows

    def finish_side(semaphore, side, rows_of):
        total = rows_of.get(0, 0)
        for distance in range(0, REACH + 1):
            if distance:
                total += rows_of.get(distance, 0)
            if total:
                pl.when(count[side] == distance)(lambda total=total: finish(semaphore, total))

    def receive(k, rows, offset, only=None):
        when_inside(offset, lambda: finish(recv_sem.at[k], rows), only)

    def receive_all(ks, rows_of):
        for side in range(2):
            finish_side(recv_sem.at[ks[side]], side, rows_of[side])

    for d in range(-REACH, REACH + 1):
        if d == 0:
            continue

        @pl.when(jnp.logical_not(inside(d)))
        def _(d=d):
            zero = jnp.zeros((ncy, ncz), F32)
            gam[REACH + d] = zero
            for step in range(3):
                ring[step, REACH + d] = zero
            for side in range(2):
                cross[REACH + d, side] = zero
            if abs(d) == 1:
                side = 0 if d < 0 else 1
                fine_zero = jnp.zeros((ny, nz), F32)
                edge = 1 if d < 0 else top
                p0[edge] = fine_zero
                beta[edge] = fine_zero
                hard[side] = fine_zero
                for step in range(2):
                    part_in[step, side] = fine_zero
                soft[side] = zero

    lane_of = lax.broadcasted_iota(jnp.int32, (nz, ncz), 0)
    block_of = lax.broadcasted_iota(jnp.int32, (nz, ncz), 1)
    for j, pick in enumerate([
        lane_of // 4 == block_of, lane_of == 4 * block_of, lane_of == 4 * block_of + 3,
    ]):
        narrow[:, j * ncz:(j + 1) * ncz] = pick.astype(F32).astype(BF16)
    one = (
        lax.broadcasted_iota(jnp.int32, (ncz, nz), 1) // 4 == lax.broadcasted_iota(jnp.int32, (ncz, nz), 0)
    ).astype(F32).astype(BF16)
    for piece in range(2):
        wide[pl.ds(piece * ncz, ncz), :] = one
    coarse_rows[...] = jnp.zeros_like(coarse_rows)
    for j in range(len(SUMS)):
        for cols in range(3):
            sums[j, cols, pl.ds(ny, 8), :] = jnp.zeros((8, ncz), F32)

    row = lax.broadcasted_iota(jnp.int32, (ny, nz), 0)
    lane = lax.broadcasted_iota(jnp.int32, (ny, nz), 1)

    def shifts(x, at_row=None, at_lane=None):
        first_row, last_row = (row == 0, row == ny - 1) if at_row is None else at_row
        first_lane, last_lane = (lane == 0, lane == nz - 1) if at_lane is None else at_lane
        return [
            jnp.where(first_row, 0.0, pltpu.roll(x, 1, 0)),
            jnp.where(last_row, 0.0, pltpu.roll(x, ny - 1, 0)),
            jnp.where(first_lane, 0.0, pltpu.roll(x, 1, 1)),
            jnp.where(last_lane, 0.0, pltpu.roll(x, nz - 1, 1)),
        ]

    def beside(x):
        up, down, left, right = shifts(x)
        return (up + down) + (left + right)

    clane = lax.broadcasted_iota(jnp.int32, (ncy, ncz), 1)

    def coarse_left(x):
        return jnp.where(clane == 0, 0.0, pltpu.roll(x, 1, 1))

    def coarse_right(x):
        return jnp.where(clane == ncz - 1, 0.0, pltpu.roll(x, ncz - 1, 1))

    def coarse_up(x):
        return pltpu.roll(x, 1, 0)

    def coarse_down(x):
        return pltpu.roll(x, ncy - 1, 0)

    def coarse_beside(x):
        return (coarse_up(x) + coarse_down(x)) + (coarse_left(x) + coarse_right(x))

    def coarsen(totals):
        pieces = [split(total) for total in totals]
        stacked = jnp.concatenate([p[0] for p in pieces] + [p[1] for p in pieces], axis=0).astype(BF16)
        product = jnp.dot(stacked, narrow[:, :ncz], preferred_element_type=F32)
        out = []
        for j in range(len(totals)):
            lower = (len(totals) + j) * ny
            slot = len(slots) % coarse_rows.shape[0]
            slots.append(slot)
            coarse_rows[slot, pl.ds(0, ny), :] = product[j * ny:(j + 1) * ny] + product[lower:lower + ny]
            parts = [coarse_rows[slot, pl.ds(k, ncy, stride=4), :] for k in range(4)]
            out.append(((parts[0] + parts[1]) + (parts[2] + parts[3])) * (1.0 / 64.0))
        return out

    slots = []

    with jax.named_scope("entry"):
        pl.semaphore_wait(barrier, 2 + neighbours)
    send(starts.at[0, 0], p0.at[top], first[1], fine, -1, t, group=early)
    send(starts.at[0, last], p0.at[1], first[0], fine, 1, t, group=early + 1)

    tell(known_sem.at[0])

    finish(load_sem, 5 * planes * fine)

    def coefficients(k):
        conduct = 1.0 / rho[k]
        mass = 1.0 + MASS_FLAG * moving[k].astype(F32)
        full = mass + 6.0 * STIFFNESS * conduct
        relax = RELAX / full
        stiff[k] = STIFFNESS * conduct
        diag[k] = full
        beta[k + 2] = (STIFFNESS * conduct) * relax
        for step in range(2):
            alpha[step, k] = (FORCE_WEIGHT * force[step, k]) * relax
        return mass, conduct

    def smooth(x, shift, i, below=True, above=True):
        here = x[i]
        around = beside(here)
        if below:
            around = around + x[i - 1]
        if above:
            around = around + x[i + 1]
        return here + (shift + beta[i] * (around - 6.0 * here))

    found = {0: coefficients(0)}
    send(beta.at[2], beta.at[top], betas[1], fine, -1, t, group=coefs, only=teller)
    found[last] = coefficients(last)
    send(beta.at[last + 2], beta.at[1], betas[0], fine, 1, t, group=coefs + 1, only=teller)
    part_out[0, 0] = smooth(p0, alpha[0, 0], 2, below=False)
    send(part_out.at[0, 0], part_in.at[0, 1], part[1], fine, -1, t, group=early)
    part_out[0, 1] = smooth(p0, alpha[0, last], last + 2, above=False)
    send(part_out.at[0, 1], part_in.at[0, 0], part[0], fine, 1, t, group=early + 1)
    for k in range(1, last):
        found[k] = coefficients(k)
        u0[k + 2] = smooth(p0, alpha[0, k], k + 2)

    mass_c = coarsen([functools.reduce(lambda a, b: a + b, [found[k][0] for k in range(planes)])])[0]
    conduct_c = coarsen([functools.reduce(lambda a, b: a + b, [found[k][1] for k in range(planes)])])[0]
    real = lax.broadcasted_iota(jnp.int32, (ncy, ncz), 0) < ny // 4
    relax_c = jnp.where(real, RELAX / jnp.where(real, mass_c + 6.0 * COARSE_STIFF * conduct_c, 1.0), 0.0)
    gam[REACH] = COARSE_STIFF * conduct_c * relax_c
    soft[2] = relax_c
    part_out[1, 0] = alpha[1, 0] + beta[2] * u0[3]
    part_out[1, 1] = alpha[1, last] + beta[last + 2] * u0[last + 1]
    pl.semaphore_wait(known_sem.at[0], neighbours)
    tell(known_sem.at[1])

    def block_sums(named):
        names = list(named)
        pieces = [split(named[name]) for name in names]
        stacked = jnp.concatenate([p[0] for p in pieces] + [p[1] for p in pieces], axis=0).astype(BF16)
        product = jnp.dot(stacked, narrow[...], preferred_element_type=F32)
        for j, name in enumerate(names):
            lower = (len(names) + j) * ny
            whole = product[j * ny:(j + 1) * ny] + product[lower:lower + ny]
            for cols in range(3):
                sums[SUMS.index(name), cols, pl.ds(0, ny), :] = whole[:, cols * ncz:(cols + 1) * ncz]

    with jax.named_scope("operator"):
        tile_rows = (row % 4 == 0, row % 4 == 3)
        tile_lanes = (lane % 4 == 0, lane % 4 == 3)
        total = {}
        for k in range(planes):
            stiff_k = stiff[k]
            up, down, left, right = shifts(stiff_k, tile_rows, tile_lanes)
            around = (up + down) + (left + right)
            if k > 0:
                around = around + stiff[k - 1]
            if k < last:
                around = around + stiff[k + 1]
            made = {"V": (1.0 - RELAX) * stiff_k + beta[k + 2] * around}
            for name, moved in zip(("ym", "yp", "zm", "zp"), shifts(beta[k + 2])):
                made[name] = stiff_k * moved
            for name, value in made.items():
                total[name] = total[name] + value if name in total else value
            if k in (0, last):
                block_sums({name + ("0" if k == 0 else "3"): value for name, value in made.items()})
        block_sums(total)
    pl.semaphore_wait(known_sem.at[1], neighbours)
    tell(known_sem.at[2])

    def residual(prior, state, source):
        total = jnp.zeros((ny, nz), F32)
        for k in range(planes):
            here = state[k + 2]
            mass = 1.0 + MASS_FLAG * moving[k].astype(F32)
            around = beside(here)
            if k > 0:
                around = around + state[k + 1]
            if k < last:
                around = around + state[k + 3]
            total = total + (mass * prior[k + 2] + FORCE_WEIGHT * source[k]) - (diag[k] * here - stiff[k] * around)
        return total

    def pass_on(part, k, side, only):
        send(part, part, k, fine, side, mate, to=me, group=told + (side > 0), only=only)

    for side in range(2):
        finish_side(send_sem.at[early + side], side, sent[early + side])
    pl.semaphore_signal(gone_sem, inc=1, device_id=(mate, me), device_id_type=MESH)
    pl.semaphore_wait(gone_sem, 1)
    send(part_out.at[1, 0], part_in.at[1, 1], further[1], fine, -1, t, group=second)
    send(part_out.at[1, 1], part_in.at[1, 0], further[0], fine, 1, t, group=second + 1)


    for side, i in ((-1, 1), (1, top)):
        receive(first[side > 0], fine, side)
        receive(betas[side > 0], fine, side, only=teller)
        pass_on(beta.at[i], passed[side > 0], side, teller)
    u0[2] = part_out[0, 0] + beta[2] * p0[1]
    u0[last + 2] = part_out[0, 1] + beta[last + 2] * p0[top]
    inner = residual(p0, u0, force.at[0])
    pl.semaphore_wait(known_sem.at[2], neighbours)
    pl.semaphore_signal(known_sem.at[3], inc=1, device_id=(behind, me), device_id_type=MESH)
    for d in order[:-2]:
        send(gam.at[REACH], gam.at[REACH - d], near[d < 0], coarse, d, t)
    send(soft.at[2], soft.at[1], near[1], coarse, -1, t)
    send(soft.at[2], soft.at[0], near[0], coarse, 1, t)
    for side, i in ((-1, 1), (1, top)):
        receive(part[side > 0], fine, side)
        receive(passed[side > 0], fine, side, only=other)
    u0[1] = part_in[0, 0] + beta[1] * p0[2]
    u0[top] = part_in[0, 1] + beta[top] * p0[last + 2]
    ring[0, REACH] = relax_c * coarsen([inner + (stiff[0] * u0[1] + stiff[last] * u0[top])])[0]
    for d in order:
        send(ring.at[0, REACH], ring.at[0, REACH - d], near[d < 0], coarse, d, t)

    for i in range(2, top):
        b1[i] = smooth(u0, alpha[1, i - 2], i)
    inner = residual(u0, b1, force.at[1])
    block_sums({"xm": stiff[0] * beta[1], "xp": stiff[last] * beta[top]})

    def block_sum(name, rows=None, lanes="all"):
        j, cols = SUMS.index(name), {"all": 0, "zm": 1, "zp": 2}[lanes]
        if rows is not None:
            return sums[j, cols, pl.ds({"ym": 0, "yp": 3}[rows], ncy, stride=4), :]
        parts = [sums[j, cols, pl.ds(k, ncy, stride=4), :] for k in range(4)]
        return (parts[0] + parts[1]) + (parts[2] + parts[3])

    with jax.named_scope("points"):
        faces, edges = {}, {}
        for f in FACES:
            if f[0] == "x":
                faces[f] = block_sum("V0" if f == "xm" else "V3") - block_sum(f)
            elif f[0] == "y":
                faces[f] = block_sum("V", rows=f) - block_sum(f, rows=f)
            else:
                faces[f] = block_sum("V", lanes=f) - block_sum(f, lanes=f)
            for d in FACES:
                if d[0] == f[0]:
                    continue
                plane = f + {"xm": "0", "xp": "3"}.get(d, "")
                pick = {a[0]: a for a in (f, d)}
                edges[f, d] = block_sum(plane, rows=pick.get("y"), lanes=pick.get("z", "all"))
        scale = relax_c * (1.0 / 64.0)
        points = {"0": -functools.reduce(lambda a, b: a + b, faces.values())}
        for f in FACES:
            points[f] = faces[f] - functools.reduce(lambda a, b: a + b, [edges[f, d] for d in FACES if d[0] != f[0]])
        for f, d in EDGES:
            points[f + d] = edges[f, d] + edges[d, f]
        for j, name in enumerate(POINTS):
            operator[j] = scale * points[name]

    def corrected(errors):
        below, here, above = errors
        moves = {"ym": coarse_up, "yp": coarse_down, "zm": coarse_left, "zp": coarse_right}
        at = {"0": here, "xm": below, "xp": above}
        for f, move in moves.items():
            at[f] = move(here)
            for x in ("xm", "xp"):
                at[x + f] = move(at[x])
        for f in ("ym", "yp"):
            for d in ("zm", "zp"):
                at[f + d] = moves[f](at[d])
        terms = [operator[j] * at[name] for j, name in enumerate(POINTS)]
        while len(terms) > 1:
            terms = [a + b for a, b in zip(terms[::2], terms[1::2])] + ([terms[-1]] if len(terms) % 2 else [])
        return terms[0]

    for side in range(2):
        finish_side(send_sem.at[second + side], side, {1: fine})
    send(stiff.at[0], hard.at[1], hards[1], fine, -1, t, group=coefs, only=other)
    send(stiff.at[last], hard.at[0], hards[0], fine, 1, t, group=coefs + 1, only=other)
    for side, i, away in ((-1, 1, 0), (1, top, 1)):
        receive(further[side > 0], fine, side)
        b1[i] = smooth(u0, part_in[1, away], i, below=side > 0, above=side < 0)
    plain = relax_c * coarsen([inner + (stiff[0] * b1[1] + stiff[last] * b1[top])])[0]
    receive_all(near, [{d: coarse * (3 if d == 1 else 2 if d < REACH else 1) for d in range(1, REACH + 1)}] * 2)

    def solve(step, width):
        right = {i: ring[step, i] for i in range(1 - width, SLOTS - 1 + width)}
        if step == 2:
            right = {i: x + (cross[i - 1, 1] + cross[i + 1, 0]) for i, x in right.items()}
        error = right
        for sweep in range(COARSE_SWEEPS - 1):
            reach = COARSE_SWEEPS - 2 - sweep + width
            error = {
                i: (1.0 - RELAX) * error[i] + right[i]
                + gam[i] * (coarse_beside(error[i]) + (error[i - 1] + error[i + 1]))
                for i in range(REACH - reach, REACH + reach + 1)
            }
        return [error[i] for i in range(REACH - width, REACH + width + 1)]

    def expanded(errors):
        for j, error in enumerate(errors):
            for k in range(4):
                spread[j, pl.ds(k, ncy, stride=4), :] = error
        tall = jnp.concatenate([spread[j, pl.ds(0, ny), :] for j in range(len(errors))], axis=0)
        stacked = jnp.concatenate(split(tall), axis=1).astype(BF16)
        product = jnp.dot(stacked, wide[...], preferred_element_type=F32)
        return [product[j * ny:(j + 1) * ny] for j in range(len(errors))]

    errors = solve(0, 1)
    own[...] = plain + corrected(errors)
    pl.semaphore_wait(known_sem.at[3], 1)
    for d in order + [0]:
        send(own, ring.at[1, REACH - d], following[d < 0], coarse, d, ahead)

    low, mid, high = expanded(errors)
    mid_change = beside(mid) - 4.0 * mid
    u1[2] = b1[2] + (mid + beta[2] * (mid_change + (low - mid)))
    for i in range(3, last + 2):
        u1[i] = b1[i] + (mid + beta[i] * mid_change)
    u1[last + 2] = b1[last + 2] + (mid + beta[last + 2] * (mid_change + (high - mid)))
    u1[1] = b1[1] + (low + beta[1] * (beside(low) - 4.0 * low + (mid - low)))
    u1[top] = b1[top] + (high + beta[top] * (beside(high) - 4.0 * high + (mid - high)))
    moved = pl.ds(1, planes + 2)
    send(u1.at[moved], came.at[moved], states, (planes + 2) * fine, 0, ahead)
    for side, i in ((-1, 0), (1, 1)):
        receive(hards[side > 0], fine, side, only=other)
        pass_on(hard.at[i], hards_passed[side > 0], side, other)
    receive(states, (planes + 2) * fine, 0)
    for i in range(2, top):
        v2[i] = smooth(came, alpha[0, i - 2], i)
    for side in (-1, 1):
        receive(hards_passed[side > 0], fine, side, only=teller)
    below, above = coarsen([hard[0] * v2[2], hard[1] * v2[last + 2]])
    cross[REACH, 0] = soft[0] * below
    cross[REACH, 1] = soft[1] * above
    for d in order:
        send(cross.at[REACH], cross.at[REACH - d], late[d < 0], 2 * coarse, d, t)
    plain = relax_c * coarsen([residual(came, v2, force.at[0])])[0]

    receive_all(following, [{d: coarse for d in range(low, REACH + 1)} for low in range(2)])
    errors = solve(1, 1)
    ring[2, REACH] = plain + corrected(errors)
    for d in order[:-2]:
        send(ring.at[2, REACH], ring.at[2, REACH - d], late[d < 0], coarse, d, t)

    low, mid, high = expanded(errors)
    change = beside(mid) - 4.0 * mid
    base_shift[...] = mid
    for k in range(planes):
        out_base[0, k] = came[k + 2]
        around = change + (low - mid) if k == 0 else change + (high - mid) if k == last else change
        out_state[0, k] = v2[k + 2] + (mid + beta[k + 2] * around)
    receive_all(late, [{d: coarse * (3 if d < REACH else 2) for d in range(1, REACH + 1)}] * 2)
    state_shift[...] = expanded(solve(2, 0))[0]
    for side in range(2):
        finish_side(send_sem.at[side], side, sent[side])
        for group in (coefs, told):
            when_inside(2 * side - 1, lambda side=side, group=group: finish(send_sem.at[group + side], fine))
    finish(send_sem.at[middle], sent[middle][0])


def solution(mesh):
    n, nt = mesh.shape["space"], mesh.shape["tm"]

    def local(slab_starts, forcing, density, moving_flags):
        _, planes, ny, nz = slab_starts.shape
        plane = (ny, nz)
        block = (planes,) + plane
        padded = (planes + 4,) + plane
        coarse = (8, nz // 4)
        result = jax.ShapeDtypeStruct(slab_starts.shape, F32)
        shift = jax.ShapeDtypeStruct(plane, F32)
        base, state, base_shift, state_shift = pl.pallas_call(
            functools.partial(kernel, n, nt, planes),
            out_shape=(result, result, shift, shift),
            in_specs=[pl.BlockSpec(memory_space=pl.ANY)] * 4,
            out_specs=(pl.BlockSpec(memory_space=pltpu.VMEM),) * 4,
            scratch_shapes=[
                pltpu.VMEM(padded, F32),
                pltpu.VMEM(padded, F32),
                pltpu.VMEM(padded, F32),
                pltpu.VMEM(padded, F32),
                pltpu.VMEM(padded, F32),
                pltpu.VMEM(padded, F32),
                pltpu.VMEM((2,) + block, F32),
                pltpu.VMEM(block, F32),
                pltpu.VMEM(block, jnp.int32),
                pltpu.VMEM(block, F32),
                pltpu.VMEM(block, F32),
                pltpu.VMEM((2,) + block, F32),
                pltpu.VMEM(padded, F32),
                pltpu.VMEM((2,) + plane, F32),
                pltpu.VMEM((2, 2) + plane, F32),
                pltpu.VMEM((2, 2) + plane, F32),
                pltpu.VMEM((3, SLOTS) + coarse, F32),
                pltpu.VMEM(coarse, F32),
                pltpu.VMEM((SLOTS, 2) + coarse, F32),
                pltpu.VMEM((SLOTS,) + coarse, F32),
                pltpu.VMEM((3,) + coarse, F32),
                pltpu.VMEM((4, 32, nz // 4), F32),
                pltpu.VMEM((len(SUMS), 3, 32, nz // 4), F32),
                pltpu.VMEM((len(POINTS),) + coarse, F32),
                pltpu.VMEM((2 * nz // 4, nz), BF16),
                pltpu.VMEM((nz, 3 * nz // 4), BF16),
                pltpu.VMEM((3, 32, nz // 4), F32),
                pltpu.VMEM((8 * planes * ny * nz // 128, 128), F32),
                pltpu.SemaphoreType.DMA,
                pltpu.SemaphoreType.REGULAR,
                pltpu.SemaphoreType.REGULAR((4,)),
                pltpu.SemaphoreType.DMA((11,)),
                pltpu.SemaphoreType.DMA((21,)),
            ],
            compiler_params=pltpu.CompilerParams(
                collective_id=0, has_side_effects=True, vmem_limit_bytes=32 * 1024 * 1024
            ),
            name="cycle",
        )(*[pltpu.with_memory_space_constraint(x, pltpu.HBM) for x in (slab_starts, forcing, density, moving_flags)])
        return base + base_shift, state + state_shift

    placed = (
        P("tm", "space", None, None),
        P("tm", None, "space", None, None),
        P("space", None, None),
        P("space", None, None),
    )
    return jax.shard_map(
        local,
        mesh=mesh,
        in_specs=placed,
        out_specs=(P("tm", "space", None, None), P("tm", "space", None, None)),
        check_vma=False,
    )
```

```python
import functools

import jax
import jax.numpy as jnp
from jax import lax
from jax.experimental import pallas as pl
from jax.experimental.pallas import tpu as pltpu
from jax.sharding import PartitionSpec as P

COARSE_SWEEPS = 4
STIFFNESS = 4.0
COARSE_STIFF = 0.25
FORCE_WEIGHT = 0.5
RELAX = 0.8
MASS_FLAG = 3.0

MESH = pl.DeviceIdType.MESH
REACH = COARSE_SWEEPS
SLOTS = 2 * REACH + 1
F32 = jnp.float32
BF16 = jnp.bfloat16

FACES = ("xm", "xp", "ym", "yp", "zm", "zp")
EDGES = [(f, d) for i, f in enumerate(FACES) for d in FACES[i + 1:] if f[0] != d[0]]
POINTS = ["0"] + list(FACES) + [f + d for f, d in EDGES]

OWN = ["V0", "V3", "V"] + [f + s for f in ("ym", "yp", "zm", "zp") for s in ("0", "3", "")]
BESIDE = ["xm", "xp"]
SUMS = OWN + BESIDE


def split(x):
    hi = x.astype(BF16).astype(F32)
    return [hi, (x - hi).astype(BF16).astype(F32)]


def kernel(
    n, nt, planes,
    starts, forcing, density, flags, out_base, out_state, base_shift, state_shift,
    p0, u0, b1, u1, came, v2, force, rho, moving, stiff, diag, alpha, beta, hard,
    part_in, part_out, ring, own, cross, gam, soft, coarse_rows, sums, operator, wide, narrow, spread, sizes,
    load_sem, gone_sem, known_sem, send_sem, recv_sem,
):
    t = lax.axis_index("tm")
    me = lax.axis_index("space")
    ahead, behind = lax.rem(t + 1, nt), lax.rem(t + nt - 1, nt)
    half = lax.rem(t, 2)
    mate = t + 1 - 2 * half
    top = planes + 2
    last = planes - 1
    ny, nz = p0.shape[-2:]
    ncy, ncz = 8, nz // 4

    def inside(offset):
        if offset < 0:
            return me >= -offset
        return me < n - offset

    order = [1, -1, 3, -3, 2, -2, 4, -4]

    barrier = pltpu.get_barrier_semaphore()
    neighbours = inside(-1).astype(jnp.int32) + inside(1).astype(jnp.int32)

    def tell(semaphore):
        for d in (1, -1):
            @pl.when(inside(d))
            def _(d=d):
                pl.semaphore_signal(semaphore, inc=1, device_id=(t, me + d), device_id_type=MESH)

    tell(barrier)
    pl.semaphore_signal(barrier, inc=1, device_id=(behind, me), device_id_type=MESH)
    pl.semaphore_signal(barrier, inc=1, device_id=(ahead, me), device_id_type=MESH)

    fine = ny * nz // 128
    coarse = ncy

    def finish(semaphore, rows):
        whole = sizes.at[pl.ds(0, rows)]
        pltpu.make_async_copy(whole, whole, semaphore).wait()

    for k, src, dst in (
        (0, starts.at[0], p0.at[pl.ds(2, planes)]), (1, density, rho), (1, flags, moving), (1, forcing.at[0], force),
    ):
        pltpu.make_async_copy(src, dst, load_sem.at[k]).start()

    count = [jnp.minimum(me, REACH), jnp.minimum(n - 1 - me, REACH)]
    betas, near, following, late = [[2 * j, 2 * j + 1] for j in range(4)]
    states, first, passed, part, further, hards, hards_passed = range(8, 15)
    middle, early, second, coefs, told = range(2, 7)
    teller = half == 1
    other = half == 0
    sent = {}

    def when_inside(offset, act, only=None):
        if offset == 0:
            act()
        else:
            pl.when(inside(offset) if only is None else jnp.logical_and(only, inside(offset)))(act)

    def send(src, dst, k, rows, offset, tm, to=None, group=None, only=None):
        group = (int(offset > 0) if offset else middle) if group is None else group
        copy = pltpu.make_async_remote_copy(
            src_ref=src, dst_ref=dst, send_sem=send_sem.at[group], recv_sem=recv_sem.at[k],
            device_id=(tm, me + offset if to is None else to), device_id_type=MESH,
        )
        when_inside(offset, lambda: copy.start(), only)
        rows_of = sent.setdefault(group, {})
        rows_of[abs(offset)] = rows_of.get(abs(offset), 0) + rows

    def finish_side(semaphore, side, rows_of):
        total = rows_of.get(0, 0)
        for distance in range(0, REACH + 1):
            if distance:
                total += rows_of.get(distance, 0)
            if total:
                pl.when(count[side] == distance)(lambda total=total: finish(semaphore, total))

    def receive(k, rows, offset, only=None):
        when_inside(offset, lambda: finish(recv_sem.at[k], rows), only)

    def finish_both(semaphore, rows, only=None):
        for sides in (1, 2):
            here = neighbours == sides
            pl.when(here if only is None else jnp.logical_and(only, here))(lambda sides=sides: finish(semaphore, sides * rows))

    def receive_all(ks, rows_of):
        for side in range(2):
            finish_side(recv_sem.at[ks[side]], side, rows_of[side])

    for d in range(-REACH, REACH + 1):
        if d == 0:
            continue

        @pl.when(jnp.logical_not(inside(d)))
        def _(d=d):
            zero = jnp.zeros((ncy, ncz), F32)
            gam[REACH + d] = zero
            for step in range(3):
                ring[step, REACH + d] = zero
            for side in range(2):
                cross[REACH + d, side] = zero
            if abs(d) == 1:
                side = 0 if d < 0 else 1
                fine_zero = jnp.zeros((ny, nz), F32)
                edge = 1 if d < 0 else top
                p0[edge] = fine_zero
                beta[edge] = fine_zero
                hard[side] = fine_zero
                for step in range(2):
                    part_in[step, side] = fine_zero
                soft[side] = zero

    lane_of = lax.broadcasted_iota(jnp.int32, (nz, ncz), 0)
    block_of = lax.broadcasted_iota(jnp.int32, (nz, ncz), 1)
    for j, pick in enumerate([
        lane_of // 4 == block_of, lane_of == 4 * block_of, lane_of == 4 * block_of + 3,
    ]):
        narrow[:, j * ncz:(j + 1) * ncz] = pick.astype(F32).astype(BF16)
    one = (
        lax.broadcasted_iota(jnp.int32, (ncz, nz), 1) // 4 == lax.broadcasted_iota(jnp.int32, (ncz, nz), 0)
    ).astype(F32).astype(BF16)
    for piece in range(2):
        wide[pl.ds(piece * ncz, ncz), :] = one
    coarse_rows[...] = jnp.zeros_like(coarse_rows)
    for j in range(len(SUMS)):
        for cols in range(3):
            sums[j, cols, pl.ds(ny, 8), :] = jnp.zeros((8, ncz), F32)

    row = lax.broadcasted_iota(jnp.int32, (ny, nz), 0)
    lane = lax.broadcasted_iota(jnp.int32, (ny, nz), 1)

    def shifts(x, at_row=None, at_lane=None):
        first_row, last_row = (row == 0, row == ny - 1) if at_row is None else at_row
        first_lane, last_lane = (lane == 0, lane == nz - 1) if at_lane is None else at_lane
        return [
            jnp.where(first_row, 0.0, pltpu.roll(x, 1, 0)),
            jnp.where(last_row, 0.0, pltpu.roll(x, ny - 1, 0)),
            jnp.where(first_lane, 0.0, pltpu.roll(x, 1, 1)),
            jnp.where(last_lane, 0.0, pltpu.roll(x, nz - 1, 1)),
        ]

    def beside(x):
        up, down, left, right = shifts(x)
        return (up + down) + (left + right)

    clane = lax.broadcasted_iota(jnp.int32, (ncy, ncz), 1)

    def coarse_left(x):
        return jnp.where(clane == 0, 0.0, pltpu.roll(x, 1, 1))

    def coarse_right(x):
        return jnp.where(clane == ncz - 1, 0.0, pltpu.roll(x, ncz - 1, 1))

    def coarse_up(x):
        return pltpu.roll(x, 1, 0)

    def coarse_down(x):
        return pltpu.roll(x, ncy - 1, 0)

    def coarse_beside(x):
        return (coarse_up(x) + coarse_down(x)) + (coarse_left(x) + coarse_right(x))

    def coarsen(totals):
        pieces = [split(total) for total in totals]
        stacked = jnp.concatenate([p[0] for p in pieces] + [p[1] for p in pieces], axis=0).astype(BF16)
        product = jnp.dot(stacked, narrow[:, :ncz], preferred_element_type=F32)
        out = []
        for j in range(len(totals)):
            lower = (len(totals) + j) * ny
            slot = len(slots) % coarse_rows.shape[0]
            slots.append(slot)
            coarse_rows[slot, pl.ds(0, ny), :] = product[j * ny:(j + 1) * ny] + product[lower:lower + ny]
            parts = [coarse_rows[slot, pl.ds(k, ncy, stride=4), :] for k in range(4)]
            out.append(((parts[0] + parts[1]) + (parts[2] + parts[3])) * (1.0 / 64.0))
        return out

    slots = []

    with jax.named_scope("entry"):
        pl.semaphore_wait(barrier, 2 + neighbours)
    finish(load_sem.at[0], planes * fine)
    send(p0.at[2], p0.at[top], first, fine, -1, t, group=early)
    send(p0.at[last + 2], p0.at[1], first, fine, 1, t, group=early)

    tell(known_sem.at[0])

    finish(load_sem.at[1], 4 * planes * fine)

    def coefficients(k):
        conduct = 1.0 / rho[k]
        mass = 1.0 + MASS_FLAG * moving[k].astype(F32)
        full = mass + 6.0 * STIFFNESS * conduct
        relax = RELAX / full
        stiff[k] = STIFFNESS * conduct
        diag[k] = full
        beta[k + 2] = (STIFFNESS * conduct) * relax
        for step in range(2):
            alpha[step, k] = (FORCE_WEIGHT * force[step, k]) * relax
        return mass, conduct

    def smooth(x, shift, i, below=True, above=True):
        here = x[i]
        around = beside(here)
        if below:
            around = around + x[i - 1]
        if above:
            around = around + x[i + 1]
        return here + (shift + beta[i] * (around - 6.0 * here))

    found = {0: coefficients(0)}
    send(beta.at[2], beta.at[top], betas[1], fine, -1, t, group=coefs, only=teller)
    found[last] = coefficients(last)
    send(beta.at[last + 2], beta.at[1], betas[0], fine, 1, t, group=coefs, only=teller)
    part_out[0, 0] = smooth(p0, alpha[0, 0], 2, below=False)
    send(part_out.at[0, 0], part_in.at[0, 1], part, fine, -1, t, group=early)
    part_out[0, 1] = smooth(p0, alpha[0, last], last + 2, above=False)
    send(part_out.at[0, 1], part_in.at[0, 0], part, fine, 1, t, group=early)
    for k in range(1, last):
        found[k] = coefficients(k)
        u0[k + 2] = smooth(p0, alpha[0, k], k + 2)

    mass_c = coarsen([functools.reduce(lambda a, b: a + b, [found[k][0] for k in range(planes)])])[0]
    conduct_c = coarsen([functools.reduce(lambda a, b: a + b, [found[k][1] for k in range(planes)])])[0]
    real = lax.broadcasted_iota(jnp.int32, (ncy, ncz), 0) < ny // 4
    relax_c = jnp.where(real, RELAX / jnp.where(real, mass_c + 6.0 * COARSE_STIFF * conduct_c, 1.0), 0.0)
    gam[REACH] = COARSE_STIFF * conduct_c * relax_c
    soft[2] = relax_c
    part_out[1, 0] = alpha[1, 0] + beta[2] * u0[3]
    part_out[1, 1] = alpha[1, last] + beta[last + 2] * u0[last + 1]
    pl.semaphore_wait(known_sem.at[0], neighbours)
    tell(known_sem.at[1])

    def block_sums(named):
        names = list(named)
        pieces = [split(named[name]) for name in names]
        stacked = jnp.concatenate([p[0] for p in pieces] + [p[1] for p in pieces], axis=0).astype(BF16)
        product = jnp.dot(stacked, narrow[...], preferred_element_type=F32)
        for j, name in enumerate(names):
            lower = (len(names) + j) * ny
            whole = product[j * ny:(j + 1) * ny] + product[lower:lower + ny]
            for cols in range(3):
                sums[SUMS.index(name), cols, pl.ds(0, ny), :] = whole[:, cols * ncz:(cols + 1) * ncz]

    with jax.named_scope("operator"):
        tile_rows = (row % 4 == 0, row % 4 == 3)
        tile_lanes = (lane % 4 == 0, lane % 4 == 3)
        total = {}
        for k in range(planes):
            stiff_k = stiff[k]
            up, down, left, right = shifts(stiff_k, tile_rows, tile_lanes)
            around = (up + down) + (left + right)
            if k > 0:
                around = around + stiff[k - 1]
            if k < last:
                around = around + stiff[k + 1]
            made = {"V": (1.0 - RELAX) * stiff_k + beta[k + 2] * around}
            for name, moved in zip(("ym", "yp", "zm", "zp"), shifts(beta[k + 2])):
                made[name] = stiff_k * moved
            for name, value in made.items():
                total[name] = total[name] + value if name in total else value
            if k in (0, last):
                block_sums({name + ("0" if k == 0 else "3"): value for name, value in made.items()})
        block_sums(total)
    pl.semaphore_wait(known_sem.at[1], neighbours)
    tell(known_sem.at[2])

    def residual(prior, state, source):
        total = jnp.zeros((ny, nz), F32)
        for k in range(planes):
            here = state[k + 2]
            mass = 1.0 + MASS_FLAG * moving[k].astype(F32)
            around = beside(here)
            if k > 0:
                around = around + state[k + 1]
            if k < last:
                around = around + state[k + 3]
            total = total + (mass * prior[k + 2] + FORCE_WEIGHT * source[k]) - (diag[k] * here - stiff[k] * around)
        return total

    def pass_on(part, k, side, only):
        send(part, part, k, fine, side, mate, to=me, group=told, only=only)

    finish_both(send_sem.at[early], 2 * fine)
    pl.semaphore_signal(gone_sem, inc=1, device_id=(mate, me), device_id_type=MESH)
    pl.semaphore_wait(gone_sem, 1)
    send(part_out.at[1, 0], part_in.at[1, 1], further, fine, -1, t, group=second)
    send(part_out.at[1, 1], part_in.at[1, 0], further, fine, 1, t, group=second)


    finish_both(recv_sem.at[first], fine)
    for side, i in ((-1, 1), (1, top)):
        receive(betas[side > 0], fine, side, only=teller)
        pass_on(beta.at[i], passed, side, teller)
    u0[2] = part_out[0, 0] + beta[2] * p0[1]
    u0[last + 2] = part_out[0, 1] + beta[last + 2] * p0[top]
    inner = residual(p0, u0, force.at[0])
    pl.semaphore_wait(known_sem.at[2], neighbours)
    pl.semaphore_signal(known_sem.at[3], inc=1, device_id=(behind, me), device_id_type=MESH)
    finish_both(recv_sem.at[part], fine)
    finish_both(recv_sem.at[passed], fine, only=other)
    u0[1] = part_in[0, 0] + beta[1] * p0[2]
    u0[top] = part_in[0, 1] + beta[top] * p0[last + 2]
    ring[0, REACH] = relax_c * coarsen([inner + (stiff[0] * u0[1] + stiff[last] * u0[top])])[0]
    for d in order:
        send(ring.at[0, REACH], ring.at[0, REACH - d], near[d < 0], coarse, d, t)
    for d in order[:-2]:
        send(gam.at[REACH], gam.at[REACH - d], near[d < 0], coarse, d, t)
    send(soft.at[2], soft.at[1], near[1], coarse, -1, t)
    send(soft.at[2], soft.at[0], near[0], coarse, 1, t)

    for i in range(2, top):
        b1[i] = smooth(u0, alpha[1, i - 2], i)
    inner = residual(u0, b1, force.at[1])
    block_sums({"xm": stiff[0] * beta[1], "xp": stiff[last] * beta[top]})

    def block_sum(name, rows=None, lanes="all"):
        j, cols = SUMS.index(name), {"all": 0, "zm": 1, "zp": 2}[lanes]
        if rows is not None:
            return sums[j, cols, pl.ds({"ym": 0, "yp": 3}[rows], ncy, stride=4), :]
        parts = [sums[j, cols, pl.ds(k, ncy, stride=4), :] for k in range(4)]
        return (parts[0] + parts[1]) + (parts[2] + parts[3])

    with jax.named_scope("points"):
        faces, edges = {}, {}
        for f in FACES:
            if f[0] == "x":
                faces[f] = block_sum("V0" if f == "xm" else "V3") - block_sum(f)
            elif f[0] == "y":
                faces[f] = block_sum("V", rows=f) - block_sum(f, rows=f)
            else:
                faces[f] = block_sum("V", lanes=f) - block_sum(f, lanes=f)
            for d in FACES:
                if d[0] == f[0]:
                    continue
                plane = f + {"xm": "0", "xp": "3"}.get(d, "")
                pick = {a[0]: a for a in (f, d)}
                edges[f, d] = block_sum(plane, rows=pick.get("y"), lanes=pick.get("z", "all"))
        scale = relax_c * (1.0 / 64.0)
        points = {"0": -functools.reduce(lambda a, b: a + b, faces.values())}
        for f in FACES:
            points[f] = faces[f] - functools.reduce(lambda a, b: a + b, [edges[f, d] for d in FACES if d[0] != f[0]])
        for f, d in EDGES:
            points[f + d] = edges[f, d] + edges[d, f]
        for j, name in enumerate(POINTS):
            operator[j] = scale * points[name]

    def corrected(errors):
        below, here, above = errors
        moves = {"ym": coarse_up, "yp": coarse_down, "zm": coarse_left, "zp": coarse_right}
        at = {"0": here, "xm": below, "xp": above}
        for f, move in moves.items():
            at[f] = move(here)
            for x in ("xm", "xp"):
                at[x + f] = move(at[x])
        for f in ("ym", "yp"):
            for d in ("zm", "zp"):
                at[f + d] = moves[f](at[d])
        terms = [operator[j] * at[name] for j, name in enumerate(POINTS)]
        while len(terms) > 1:
            terms = [a + b for a, b in zip(terms[::2], terms[1::2])] + ([terms[-1]] if len(terms) % 2 else [])
        return terms[0]

    finish_both(send_sem.at[second], fine)
    send(stiff.at[0], hard.at[1], hards, fine, -1, t, group=coefs, only=other)
    send(stiff.at[last], hard.at[0], hards, fine, 1, t, group=coefs, only=other)
    finish_both(recv_sem.at[further], fine)
    for side, i, away in ((-1, 1, 0), (1, top, 1)):
        b1[i] = smooth(u0, part_in[1, away], i, below=side > 0, above=side < 0)
    plain = relax_c * coarsen([inner + (stiff[0] * b1[1] + stiff[last] * b1[top])])[0]
    receive_all(near, [{d: coarse * (3 if d == 1 else 2 if d < REACH else 1) for d in range(1, REACH + 1)}] * 2)

    def solve(step, width):
        right = {i: ring[step, i] for i in range(1 - width, SLOTS - 1 + width)}
        if step == 2:
            right = {i: x + (cross[i - 1, 1] + cross[i + 1, 0]) for i, x in right.items()}
        error = right
        for sweep in range(COARSE_SWEEPS - 1):
            reach = COARSE_SWEEPS - 2 - sweep + width
            error = {
                i: (1.0 - RELAX) * error[i] + right[i]
                + gam[i] * (coarse_beside(error[i]) + (error[i - 1] + error[i + 1]))
                for i in range(REACH - reach, REACH + reach + 1)
            }
        return [error[i] for i in range(REACH - width, REACH + width + 1)]

    def expanded(errors):
        for j, error in enumerate(errors):
            for k in range(4):
                spread[j, pl.ds(k, ncy, stride=4), :] = error
        tall = jnp.concatenate([spread[j, pl.ds(0, ny), :] for j in range(len(errors))], axis=0)
        stacked = jnp.concatenate(split(tall), axis=1).astype(BF16)
        product = jnp.dot(stacked, wide[...], preferred_element_type=F32)
        return [product[j * ny:(j + 1) * ny] for j in range(len(errors))]

    errors = solve(0, 1)
    own[...] = plain + corrected(errors)
    pl.semaphore_wait(known_sem.at[3], 1)
    for d in order + [0]:
        send(own, ring.at[1, REACH - d], following[d < 0], coarse, d, ahead)

    low, mid, high = expanded(errors)
    mid_change = beside(mid) - 4.0 * mid
    u1[2] = b1[2] + (mid + beta[2] * (mid_change + (low - mid)))
    for i in range(3, last + 2):
        u1[i] = b1[i] + (mid + beta[i] * mid_change)
    u1[last + 2] = b1[last + 2] + (mid + beta[last + 2] * (mid_change + (high - mid)))
    u1[1] = b1[1] + (low + beta[1] * (beside(low) - 4.0 * low + (mid - low)))
    u1[top] = b1[top] + (high + beta[top] * (beside(high) - 4.0 * high + (mid - high)))
    moved = pl.ds(1, planes + 2)
    send(u1.at[moved], came.at[moved], states, (planes + 2) * fine, 0, ahead)
    finish_both(recv_sem.at[hards], fine, only=other)
    for side, i in ((-1, 0), (1, 1)):
        pass_on(hard.at[i], hards_passed, side, other)
    receive(states, (planes + 2) * fine, 0)
    for i in range(2, top):
        v2[i] = smooth(came, alpha[0, i - 2], i)
    finish_both(recv_sem.at[hards_passed], fine, only=teller)
    below, above = coarsen([hard[0] * v2[2], hard[1] * v2[last + 2]])
    cross[REACH, 0] = soft[0] * below
    cross[REACH, 1] = soft[1] * above
    for d in order:
        send(cross.at[REACH], cross.at[REACH - d], late[d < 0], 2 * coarse, d, t)
    plain = relax_c * coarsen([residual(came, v2, force.at[0])])[0]

    receive_all(following, [{d: coarse for d in range(low, REACH + 1)} for low in range(2)])
    errors = solve(1, 1)
    ring[2, REACH] = plain + corrected(errors)
    for d in order[:-2]:
        send(ring.at[2, REACH], ring.at[2, REACH - d], late[d < 0], coarse, d, t)

    low, mid, high = expanded(errors)
    change = beside(mid) - 4.0 * mid
    base_shift[...] = mid
    for k in range(planes):
        out_base[0, k] = came[k + 2]
        around = change + (low - mid) if k == 0 else change + (high - mid) if k == last else change
        out_state[0, k] = v2[k + 2] + (mid + beta[k + 2] * around)
    receive_all(late, [{d: coarse * (3 if d < REACH else 2) for d in range(1, REACH + 1)}] * 2)
    state_shift[...] = expanded(solve(2, 0))[0]
    for side in range(2):
        finish_side(send_sem.at[side], side, sent[side])
    finish_both(send_sem.at[coefs], fine)
    finish_both(send_sem.at[told], fine)
    finish(send_sem.at[middle], sent[middle][0])


def solution(mesh):
    n, nt = mesh.shape["space"], mesh.shape["tm"]

    def local(slab_starts, forcing, density, moving_flags):
        _, planes, ny, nz = slab_starts.shape
        plane = (ny, nz)
        block = (planes,) + plane
        padded = (planes + 4,) + plane
        coarse = (8, nz // 4)
        result = jax.ShapeDtypeStruct(slab_starts.shape, F32)
        shift = jax.ShapeDtypeStruct(plane, F32)
        base, state, base_shift, state_shift = pl.pallas_call(
            functools.partial(kernel, n, nt, planes),
            out_shape=(result, result, shift, shift),
            in_specs=[pl.BlockSpec(memory_space=pl.ANY)] * 4,
            out_specs=(pl.BlockSpec(memory_space=pltpu.VMEM),) * 4,
            scratch_shapes=[
                pltpu.VMEM(padded, F32),
                pltpu.VMEM(padded, F32),
                pltpu.VMEM(padded, F32),
                pltpu.VMEM(padded, F32),
                pltpu.VMEM(padded, F32),
                pltpu.VMEM(padded, F32),
                pltpu.VMEM((2,) + block, F32),
                pltpu.VMEM(block, F32),
                pltpu.VMEM(block, jnp.int32),
                pltpu.VMEM(block, F32),
                pltpu.VMEM(block, F32),
                pltpu.VMEM((2,) + block, F32),
                pltpu.VMEM(padded, F32),
                pltpu.VMEM((2,) + plane, F32),
                pltpu.VMEM((2, 2) + plane, F32),
                pltpu.VMEM((2, 2) + plane, F32),
                pltpu.VMEM((3, SLOTS) + coarse, F32),
                pltpu.VMEM(coarse, F32),
                pltpu.VMEM((SLOTS, 2) + coarse, F32),
                pltpu.VMEM((SLOTS,) + coarse, F32),
                pltpu.VMEM((3,) + coarse, F32),
                pltpu.VMEM((4, 32, nz // 4), F32),
                pltpu.VMEM((len(SUMS), 3, 32, nz // 4), F32),
                pltpu.VMEM((len(POINTS),) + coarse, F32),
                pltpu.VMEM((2 * nz // 4, nz), BF16),
                pltpu.VMEM((nz, 3 * nz // 4), BF16),
                pltpu.VMEM((3, 32, nz // 4), F32),
                pltpu.VMEM((8 * planes * ny * nz // 128, 128), F32),
                pltpu.SemaphoreType.DMA((2,)),
                pltpu.SemaphoreType.REGULAR,
                pltpu.SemaphoreType.REGULAR((4,)),
                pltpu.SemaphoreType.DMA((7,)),
                pltpu.SemaphoreType.DMA((15,)),
            ],
            compiler_params=pltpu.CompilerParams(
                collective_id=0, has_side_effects=True, vmem_limit_bytes=32 * 1024 * 1024
            ),
            name="cycle",
        )(*[pltpu.with_memory_space_constraint(x, pltpu.HBM) for x in (slab_starts, forcing, density, moving_flags)])
        return base + base_shift, state + state_shift

    placed = (
        P("tm", "space", None, None),
        P("tm", None, "space", None, None),
        P("space", None, None),
        P("space", None, None),
    )
    return jax.shard_map(
        local,
        mesh=mesh,
        in_specs=placed,
        out_specs=(P("tm", "space", None, None), P("tm", "space", None, None)),
        check_vma=False,
    )
```

```python
import functools

import jax
import jax.numpy as jnp
from jax import lax
from jax.experimental import pallas as pl
from jax.experimental.pallas import tpu as pltpu
from jax.sharding import PartitionSpec as P

COARSE_SWEEPS = 4
STIFFNESS = 4.0
COARSE_STIFF = 0.25
FORCE_WEIGHT = 0.5
RELAX = 0.8
MASS_FLAG = 3.0

MESH = pl.DeviceIdType.MESH
REACH = COARSE_SWEEPS
SLOTS = 2 * REACH + 1
F32 = jnp.float32
BF16 = jnp.bfloat16

FACES = ("xm", "xp", "ym", "yp", "zm", "zp")
EDGES = [(f, d) for i, f in enumerate(FACES) for d in FACES[i + 1:] if f[0] != d[0]]
POINTS = ["0"] + list(FACES) + [f + d for f, d in EDGES]

OWN = ["V0", "V3", "V"] + [f + s for f in ("ym", "yp", "zm", "zp") for s in ("0", "3", "")]
BESIDE = ["xm", "xp"]
SUMS = OWN + BESIDE


def split(x):
    hi = x.astype(BF16).astype(F32)
    return [hi, (x - hi).astype(BF16).astype(F32)]


def kernel(
    n, nt, planes,
    starts, forcing, density, flags, out_base, out_state, base_shift, state_shift,
    p0, u0, b1, u1, came, v2, force, rho, moving, stiff, diag, alpha, beta, hard,
    part_in, part_out, ring, own, cross, gam, soft, coarse_rows, sums, operator, wide, narrow, spread, sizes,
    load_sem, gone_sem, known_sem, send_sem, recv_sem,
):
    t = lax.axis_index("tm")
    me = lax.axis_index("space")
    ahead, behind = lax.rem(t + 1, nt), lax.rem(t + nt - 1, nt)
    half = lax.rem(t, 2)
    mate = t + 1 - 2 * half
    top = planes + 2
    last = planes - 1
    ny, nz = p0.shape[-2:]
    ncy, ncz = 8, nz // 4

    def inside(offset):
        if offset < 0:
            return me >= -offset
        return me < n - offset

    order = [-3, 3, -1, 1, -2, 2, -4, 4]

    barrier = pltpu.get_barrier_semaphore()
    neighbours = inside(-1).astype(jnp.int32) + inside(1).astype(jnp.int32)

    def tell(semaphore):
        for d in (1, -1):
            @pl.when(inside(d))
            def _(d=d):
                pl.semaphore_signal(semaphore, inc=1, device_id=(t, me + d), device_id_type=MESH)

    tell(barrier)
    pl.semaphore_signal(barrier, inc=1, device_id=(behind, me), device_id_type=MESH)
    pl.semaphore_signal(barrier, inc=1, device_id=(ahead, me), device_id_type=MESH)

    fine = ny * nz // 128
    coarse = ncy

    def finish(semaphore, rows):
        whole = sizes.at[pl.ds(0, rows)]
        pltpu.make_async_copy(whole, whole, semaphore).wait()

    for k, src, dst in (
        (0, starts.at[0], p0.at[pl.ds(2, planes)]), (1, density, rho), (1, flags, moving), (1, forcing.at[0], force),
    ):
        pltpu.make_async_copy(src, dst, load_sem.at[k]).start()

    count = [jnp.minimum(me, REACH), jnp.minimum(n - 1 - me, REACH)]
    betas, near, following, late = [[2 * j, 2 * j + 1] for j in range(4)]
    states, first, passed, part, further, hards, hards_passed = range(8, 15)
    middle, early, second, coefs, told = range(2, 7)
    teller = half == 1
    other = half == 0
    sent = {}

    def when_inside(offset, act, only=None):
        if offset == 0:
            act()
        else:
            pl.when(inside(offset) if only is None else jnp.logical_and(only, inside(offset)))(act)

    def send(src, dst, k, rows, offset, tm, to=None, group=None, only=None):
        group = (int(offset > 0) if offset else middle) if group is None else group
        copy = pltpu.make_async_remote_copy(
            src_ref=src, dst_ref=dst, send_sem=send_sem.at[group], recv_sem=recv_sem.at[k],
            device_id=(tm, me + offset if to is None else to), device_id_type=MESH,
        )
        when_inside(offset, lambda: copy.start(), only)
        rows_of = sent.setdefault(group, {})
        rows_of[abs(offset)] = rows_of.get(abs(offset), 0) + rows

    def finish_side(semaphore, side, rows_of):
        total = rows_of.get(0, 0)
        for distance in range(0, REACH + 1):
            if distance:
                total += rows_of.get(distance, 0)
            if total:
                pl.when(count[side] == distance)(lambda total=total: finish(semaphore, total))

    def receive(k, rows, offset, only=None):
        when_inside(offset, lambda: finish(recv_sem.at[k], rows), only)

    def finish_both(semaphore, rows, only=None):
        for sides in (1, 2):
            here = neighbours == sides
            pl.when(here if only is None else jnp.logical_and(only, here))(lambda sides=sides: finish(semaphore, sides * rows))

    def receive_all(ks, rows_of):
        for side in range(2):
            finish_side(recv_sem.at[ks[side]], side, rows_of[side])

    for d in range(-REACH, REACH + 1):
        if d == 0:
            continue

        @pl.when(jnp.logical_not(inside(d)))
        def _(d=d):
            zero = jnp.zeros((ncy, ncz), F32)
            gam[REACH + d] = zero
            for step in range(3):
                ring[step, REACH + d] = zero
            for side in range(2):
                cross[REACH + d, side] = zero
            if abs(d) == 1:
                side = 0 if d < 0 else 1
                fine_zero = jnp.zeros((ny, nz), F32)
                edge = 1 if d < 0 else top
                p0[edge] = fine_zero
                beta[edge] = fine_zero
                hard[side] = fine_zero
                for step in range(2):
                    part_in[step, side] = fine_zero
                soft[side] = zero

    lane_of = lax.broadcasted_iota(jnp.int32, (nz, ncz), 0)
    block_of = lax.broadcasted_iota(jnp.int32, (nz, ncz), 1)
    for j, pick in enumerate([
        lane_of // 4 == block_of, lane_of == 4 * block_of, lane_of == 4 * block_of + 3,
    ]):
        narrow[:, j * ncz:(j + 1) * ncz] = pick.astype(F32).astype(BF16)
    one = (
        lax.broadcasted_iota(jnp.int32, (ncz, nz), 1) // 4 == lax.broadcasted_iota(jnp.int32, (ncz, nz), 0)
    ).astype(F32).astype(BF16)
    for piece in range(2):
        wide[pl.ds(piece * ncz, ncz), :] = one
    coarse_rows[...] = jnp.zeros_like(coarse_rows)
    for j in range(len(SUMS)):
        for cols in range(3):
            sums[j, cols, pl.ds(ny, 8), :] = jnp.zeros((8, ncz), F32)

    row = lax.broadcasted_iota(jnp.int32, (ny, nz), 0)
    lane = lax.broadcasted_iota(jnp.int32, (ny, nz), 1)

    def shifts(x, at_row=None, at_lane=None):
        first_row, last_row = (row == 0, row == ny - 1) if at_row is None else at_row
        first_lane, last_lane = (lane == 0, lane == nz - 1) if at_lane is None else at_lane
        return [
            jnp.where(first_row, 0.0, pltpu.roll(x, 1, 0)),
            jnp.where(last_row, 0.0, pltpu.roll(x, ny - 1, 0)),
            jnp.where(first_lane, 0.0, pltpu.roll(x, 1, 1)),
            jnp.where(last_lane, 0.0, pltpu.roll(x, nz - 1, 1)),
        ]

    def beside(x):
        up, down, left, right = shifts(x)
        return (up + down) + (left + right)

    clane = lax.broadcasted_iota(jnp.int32, (ncy, ncz), 1)

    def coarse_left(x):
        return jnp.where(clane == 0, 0.0, pltpu.roll(x, 1, 1))

    def coarse_right(x):
        return jnp.where(clane == ncz - 1, 0.0, pltpu.roll(x, ncz - 1, 1))

    def coarse_up(x):
        return pltpu.roll(x, 1, 0)

    def coarse_down(x):
        return pltpu.roll(x, ncy - 1, 0)

    def coarse_beside(x):
        return (coarse_up(x) + coarse_down(x)) + (coarse_left(x) + coarse_right(x))

    def coarsen(totals):
        pieces = [split(total) for total in totals]
        stacked = jnp.concatenate([p[0] for p in pieces] + [p[1] for p in pieces], axis=0).astype(BF16)
        product = jnp.dot(stacked, narrow[:, :ncz], preferred_element_type=F32)
        out = []
        for j in range(len(totals)):
            lower = (len(totals) + j) * ny
            slot = len(slots) % coarse_rows.shape[0]
            slots.append(slot)
            coarse_rows[slot, pl.ds(0, ny), :] = product[j * ny:(j + 1) * ny] + product[lower:lower + ny]
            parts = [coarse_rows[slot, pl.ds(k, ncy, stride=4), :] for k in range(4)]
            out.append(((parts[0] + parts[1]) + (parts[2] + parts[3])) * (1.0 / 64.0))
        return out

    slots = []

    with jax.named_scope("entry"):
        pl.semaphore_wait(barrier, 2 + neighbours)
    finish(load_sem.at[0], planes * fine)
    send(p0.at[2], p0.at[top], first, fine, -1, t, group=early)
    send(p0.at[last + 2], p0.at[1], first, fine, 1, t, group=early)

    tell(known_sem.at[0])

    finish(load_sem.at[1], 4 * planes * fine)

    def coefficients(k):
        conduct = 1.0 / rho[k]
        mass = 1.0 + MASS_FLAG * moving[k].astype(F32)
        full = mass + 6.0 * STIFFNESS * conduct
        relax = RELAX / full
        stiff[k] = STIFFNESS * conduct
        diag[k] = full
        beta[k + 2] = (STIFFNESS * conduct) * relax
        for step in range(2):
            alpha[step, k] = (FORCE_WEIGHT * force[step, k]) * relax
        return mass, conduct

    def smooth(x, shift, i, below=True, above=True):
        here = x[i]
        around = beside(here)
        if below:
            around = around + x[i - 1]
        if above:
            around = around + x[i + 1]
        return here + (shift + beta[i] * (around - 6.0 * here))

    found = {0: coefficients(0)}
    send(beta.at[2], beta.at[top], betas[1], fine, -1, t, group=coefs, only=teller)
    found[last] = coefficients(last)
    send(beta.at[last + 2], beta.at[1], betas[0], fine, 1, t, group=coefs, only=teller)
    part_out[0, 0] = smooth(p0, alpha[0, 0], 2, below=False)
    send(part_out.at[0, 0], part_in.at[0, 1], part, fine, -1, t, group=early)
    part_out[0, 1] = smooth(p0, alpha[0, last], last + 2, above=False)
    send(part_out.at[0, 1], part_in.at[0, 0], part, fine, 1, t, group=early)
    for k in range(1, last):
        found[k] = coefficients(k)
        u0[k + 2] = smooth(p0, alpha[0, k], k + 2)

    mass_c = coarsen([functools.reduce(lambda a, b: a + b, [found[k][0] for k in range(planes)])])[0]
    conduct_c = coarsen([functools.reduce(lambda a, b: a + b, [found[k][1] for k in range(planes)])])[0]
    real = lax.broadcasted_iota(jnp.int32, (ncy, ncz), 0) < ny // 4
    relax_c = jnp.where(real, RELAX / jnp.where(real, mass_c + 6.0 * COARSE_STIFF * conduct_c, 1.0), 0.0)
    gam[REACH] = COARSE_STIFF * conduct_c * relax_c
    soft[2] = relax_c
    part_out[1, 0] = alpha[1, 0] + beta[2] * u0[3]
    part_out[1, 1] = alpha[1, last] + beta[last + 2] * u0[last + 1]
    pl.semaphore_wait(known_sem.at[0], neighbours)
    tell(known_sem.at[1])

    def block_sums(named):
        names = list(named)
        pieces = [split(named[name]) for name in names]
        stacked = jnp.concatenate([p[0] for p in pieces] + [p[1] for p in pieces], axis=0).astype(BF16)
        product = jnp.dot(stacked, narrow[...], preferred_element_type=F32)
        for j, name in enumerate(names):
            lower = (len(names) + j) * ny
            whole = product[j * ny:(j + 1) * ny] + product[lower:lower + ny]
            for cols in range(3):
                sums[SUMS.index(name), cols, pl.ds(0, ny), :] = whole[:, cols * ncz:(cols + 1) * ncz]

    with jax.named_scope("operator"):
        tile_rows = (row % 4 == 0, row % 4 == 3)
        tile_lanes = (lane % 4 == 0, lane % 4 == 3)
        total = {}
        for k in range(planes):
            stiff_k = stiff[k]
            up, down, left, right = shifts(stiff_k, tile_rows, tile_lanes)
            around = (up + down) + (left + right)
            if k > 0:
                around = around + stiff[k - 1]
            if k < last:
                around = around + stiff[k + 1]
            made = {"V": (1.0 - RELAX) * stiff_k + beta[k + 2] * around}
            for name, moved in zip(("ym", "yp", "zm", "zp"), shifts(beta[k + 2])):
                made[name] = stiff_k * moved
            for name, value in made.items():
                total[name] = total[name] + value if name in total else value
            if k in (0, last):
                block_sums({name + ("0" if k == 0 else "3"): value for name, value in made.items()})
        block_sums(total)
    pl.semaphore_wait(known_sem.at[1], neighbours)
    tell(known_sem.at[2])

    def residual(prior, state, source):
        total = jnp.zeros((ny, nz), F32)
        for k in range(planes):
            here = state[k + 2]
            mass = 1.0 + MASS_FLAG * moving[k].astype(F32)
            around = beside(here)
            if k > 0:
                around = around + state[k + 1]
            if k < last:
                around = around + state[k + 3]
            total = total + (mass * prior[k + 2] + FORCE_WEIGHT * source[k]) - (diag[k] * here - stiff[k] * around)
        return total

    def pass_on(part, k, side, only):
        send(part, part, k, fine, side, mate, to=me, group=told, only=only)

    finish_both(send_sem.at[early], 2 * fine)
    pl.semaphore_signal(gone_sem, inc=1, device_id=(mate, me), device_id_type=MESH)
    pl.semaphore_wait(gone_sem, 1)
    send(part_out.at[1, 0], part_in.at[1, 1], further, fine, -1, t, group=second)
    send(part_out.at[1, 1], part_in.at[1, 0], further, fine, 1, t, group=second)


    finish_both(recv_sem.at[first], fine)
    for side, i in ((-1, 1), (1, top)):
        receive(betas[side > 0], fine, side, only=teller)
        pass_on(beta.at[i], passed, side, teller)
    u0[2] = part_out[0, 0] + beta[2] * p0[1]
    u0[last + 2] = part_out[0, 1] + beta[last + 2] * p0[top]
    inner = residual(p0, u0, force.at[0])
    pl.semaphore_wait(known_sem.at[2], neighbours)
    pl.semaphore_signal(known_sem.at[3], inc=1, device_id=(behind, me), device_id_type=MESH)
    finish_both(recv_sem.at[part], fine)
    finish_both(recv_sem.at[passed], fine, only=other)
    u0[1] = part_in[0, 0] + beta[1] * p0[2]
    u0[top] = part_in[0, 1] + beta[top] * p0[last + 2]
    ring[0, REACH] = relax_c * coarsen([inner + (stiff[0] * u0[1] + stiff[last] * u0[top])])[0]
    for d in order:
        send(ring.at[0, REACH], ring.at[0, REACH - d], near[d < 0], coarse, d, t)
    for d in order[:-2]:
        send(gam.at[REACH], gam.at[REACH - d], near[d < 0], coarse, d, t)
    send(soft.at[2], soft.at[1], near[1], coarse, -1, t)
    send(soft.at[2], soft.at[0], near[0], coarse, 1, t)

    for i in range(2, top):
        b1[i] = smooth(u0, alpha[1, i - 2], i)
    inner = residual(u0, b1, force.at[1])
    block_sums({"xm": stiff[0] * beta[1], "xp": stiff[last] * beta[top]})

    def block_sum(name, rows=None, lanes="all"):
        j, cols = SUMS.index(name), {"all": 0, "zm": 1, "zp": 2}[lanes]
        if rows is not None:
            return sums[j, cols, pl.ds({"ym": 0, "yp": 3}[rows], ncy, stride=4), :]
        parts = [sums[j, cols, pl.ds(k, ncy, stride=4), :] for k in range(4)]
        return (parts[0] + parts[1]) + (parts[2] + parts[3])

    with jax.named_scope("points"):
        faces, edges = {}, {}
        for f in FACES:
            if f[0] == "x":
                faces[f] = block_sum("V0" if f == "xm" else "V3") - block_sum(f)
            elif f[0] == "y":
                faces[f] = block_sum("V", rows=f) - block_sum(f, rows=f)
            else:
                faces[f] = block_sum("V", lanes=f) - block_sum(f, lanes=f)
            for d in FACES:
                if d[0] == f[0]:
                    continue
                plane = f + {"xm": "0", "xp": "3"}.get(d, "")
                pick = {a[0]: a for a in (f, d)}
                edges[f, d] = block_sum(plane, rows=pick.get("y"), lanes=pick.get("z", "all"))
        scale = relax_c * (1.0 / 64.0)
        points = {"0": -functools.reduce(lambda a, b: a + b, faces.values())}
        for f in FACES:
            points[f] = faces[f] - functools.reduce(lambda a, b: a + b, [edges[f, d] for d in FACES if d[0] != f[0]])
        for f, d in EDGES:
            points[f + d] = edges[f, d] + edges[d, f]
        for j, name in enumerate(POINTS):
            operator[j] = scale * points[name]

    def corrected(errors):
        below, here, above = errors
        moves = {"ym": coarse_up, "yp": coarse_down, "zm": coarse_left, "zp": coarse_right}
        at = {"0": here, "xm": below, "xp": above}
        for f, move in moves.items():
            at[f] = move(here)
            for x in ("xm", "xp"):
                at[x + f] = move(at[x])
        for f in ("ym", "yp"):
            for d in ("zm", "zp"):
                at[f + d] = moves[f](at[d])
        terms = [operator[j] * at[name] for j, name in enumerate(POINTS)]
        while len(terms) > 1:
            terms = [a + b for a, b in zip(terms[::2], terms[1::2])] + ([terms[-1]] if len(terms) % 2 else [])
        return terms[0]

    finish_both(send_sem.at[second], fine)
    send(stiff.at[0], hard.at[1], hards, fine, -1, t, group=coefs, only=other)
    send(stiff.at[last], hard.at[0], hards, fine, 1, t, group=coefs, only=other)
    finish_both(recv_sem.at[further], fine)
    for side, i, away in ((-1, 1, 0), (1, top, 1)):
        b1[i] = smooth(u0, part_in[1, away], i, below=side > 0, above=side < 0)
    plain = relax_c * coarsen([inner + (stiff[0] * b1[1] + stiff[last] * b1[top])])[0]
    receive_all(near, [{d: coarse * (3 if d == 1 else 2 if d < REACH else 1) for d in range(1, REACH + 1)}] * 2)

    def solve(step, width):
        right = {i: ring[step, i] for i in range(1 - width, SLOTS - 1 + width)}
        if step == 2:
            right = {i: x + (cross[i - 1, 1] + cross[i + 1, 0]) for i, x in right.items()}
        error = right
        for sweep in range(COARSE_SWEEPS - 1):
            reach = COARSE_SWEEPS - 2 - sweep + width
            error = {
                i: (1.0 - RELAX) * error[i] + right[i]
                + gam[i] * (coarse_beside(error[i]) + (error[i - 1] + error[i + 1]))
                for i in range(REACH - reach, REACH + reach + 1)
            }
        return [error[i] for i in range(REACH - width, REACH + width + 1)]

    def expanded(errors):
        for j, error in enumerate(errors):
            for k in range(4):
                spread[j, pl.ds(k, ncy, stride=4), :] = error
        tall = jnp.concatenate([spread[j, pl.ds(0, ny), :] for j in range(len(errors))], axis=0)
        stacked = jnp.concatenate(split(tall), axis=1).astype(BF16)
        product = jnp.dot(stacked, wide[...], preferred_element_type=F32)
        return [product[j * ny:(j + 1) * ny] for j in range(len(errors))]

    errors = solve(0, 1)
    own[...] = plain + corrected(errors)
    pl.semaphore_wait(known_sem.at[3], 1)
    for d in order + [0]:
        send(own, ring.at[1, REACH - d], following[d < 0], coarse, d, ahead)

    low, mid, high = expanded(errors)
    mid_change = beside(mid) - 4.0 * mid
    u1[2] = b1[2] + (mid + beta[2] * (mid_change + (low - mid)))
    for i in range(3, last + 2):
        u1[i] = b1[i] + (mid + beta[i] * mid_change)
    u1[last + 2] = b1[last + 2] + (mid + beta[last + 2] * (mid_change + (high - mid)))
    u1[1] = b1[1] + (low + beta[1] * (beside(low) - 4.0 * low + (mid - low)))
    u1[top] = b1[top] + (high + beta[top] * (beside(high) - 4.0 * high + (mid - high)))
    moved = pl.ds(1, planes + 2)
    send(u1.at[moved], came.at[moved], states, (planes + 2) * fine, 0, ahead)
    finish_both(recv_sem.at[hards], fine, only=other)
    for side, i in ((-1, 0), (1, 1)):
        pass_on(hard.at[i], hards_passed, side, other)
    receive(states, (planes + 2) * fine, 0)
    for i in range(2, top):
        v2[i] = smooth(came, alpha[0, i - 2], i)
    finish_both(recv_sem.at[hards_passed], fine, only=teller)
    below, above = coarsen([hard[0] * v2[2], hard[1] * v2[last + 2]])
    cross[REACH, 0] = soft[0] * below
    cross[REACH, 1] = soft[1] * above
    for d in order:
        send(cross.at[REACH], cross.at[REACH - d], late[d < 0], 2 * coarse, d, t)
    plain = relax_c * coarsen([residual(came, v2, force.at[0])])[0]

    receive_all(following, [{d: coarse for d in range(low, REACH + 1)} for low in range(2)])
    errors = solve(1, 1)
    ring[2, REACH] = plain + corrected(errors)
    for d in order[:-2]:
        send(ring.at[2, REACH], ring.at[2, REACH - d], late[d < 0], coarse, d, t)

    low, mid, high = expanded(errors)
    change = beside(mid) - 4.0 * mid
    base_shift[...] = mid
    for k in range(planes):
        out_base[0, k] = came[k + 2]
        around = change + (low - mid) if k == 0 else change + (high - mid) if k == last else change
        out_state[0, k] = v2[k + 2] + (mid + beta[k + 2] * around)
    receive_all(late, [{d: coarse * (3 if d < REACH else 2) for d in range(1, REACH + 1)}] * 2)
    state_shift[...] = expanded(solve(2, 0))[0]
    for side in range(2):
        finish_side(send_sem.at[side], side, sent[side])
    finish_both(send_sem.at[coefs], fine)
    finish_both(send_sem.at[told], fine)
    finish(send_sem.at[middle], sent[middle][0])


def solution(mesh):
    n, nt = mesh.shape["space"], mesh.shape["tm"]

    def local(slab_starts, forcing, density, moving_flags):
        _, planes, ny, nz = slab_starts.shape
        plane = (ny, nz)
        block = (planes,) + plane
        padded = (planes + 4,) + plane
        coarse = (8, nz // 4)
        result = jax.ShapeDtypeStruct(slab_starts.shape, F32)
        shift = jax.ShapeDtypeStruct(plane, F32)
        base, state, base_shift, state_shift = pl.pallas_call(
            functools.partial(kernel, n, nt, planes),
            out_shape=(result, result, shift, shift),
            in_specs=[pl.BlockSpec(memory_space=pl.ANY)] * 4,
            out_specs=(pl.BlockSpec(memory_space=pltpu.VMEM),) * 4,
            scratch_shapes=[
                pltpu.VMEM(padded, F32),
                pltpu.VMEM(padded, F32),
                pltpu.VMEM(padded, F32),
                pltpu.VMEM(padded, F32),
                pltpu.VMEM(padded, F32),
                pltpu.VMEM(padded, F32),
                pltpu.VMEM((2,) + block, F32),
                pltpu.VMEM(block, F32),
                pltpu.VMEM(block, jnp.int32),
                pltpu.VMEM(block, F32),
                pltpu.VMEM(block, F32),
                pltpu.VMEM((2,) + block, F32),
                pltpu.VMEM(padded, F32),
                pltpu.VMEM((2,) + plane, F32),
                pltpu.VMEM((2, 2) + plane, F32),
                pltpu.VMEM((2, 2) + plane, F32),
                pltpu.VMEM((3, SLOTS) + coarse, F32),
                pltpu.VMEM(coarse, F32),
                pltpu.VMEM((SLOTS, 2) + coarse, F32),
                pltpu.VMEM((SLOTS,) + coarse, F32),
                pltpu.VMEM((3,) + coarse, F32),
                pltpu.VMEM((4, 32, nz // 4), F32),
                pltpu.VMEM((len(SUMS), 3, 32, nz // 4), F32),
                pltpu.VMEM((len(POINTS),) + coarse, F32),
                pltpu.VMEM((2 * nz // 4, nz), BF16),
                pltpu.VMEM((nz, 3 * nz // 4), BF16),
                pltpu.VMEM((3, 32, nz // 4), F32),
                pltpu.VMEM((8 * planes * ny * nz // 128, 128), F32),
                pltpu.SemaphoreType.DMA((2,)),
                pltpu.SemaphoreType.REGULAR,
                pltpu.SemaphoreType.REGULAR((4,)),
                pltpu.SemaphoreType.DMA((7,)),
                pltpu.SemaphoreType.DMA((15,)),
            ],
            compiler_params=pltpu.CompilerParams(
                collective_id=0, has_side_effects=True, vmem_limit_bytes=32 * 1024 * 1024
            ),
            name="cycle",
        )(*[pltpu.with_memory_space_constraint(x, pltpu.HBM) for x in (slab_starts, forcing, density, moving_flags)])
        return base + base_shift, state + state_shift

    placed = (
        P("tm", "space", None, None),
        P("tm", None, "space", None, None),
        P("space", None, None),
        P("space", None, None),
    )
    return jax.shard_map(
        local,
        mesh=mesh,
        in_specs=placed,
        out_specs=(P("tm", "space", None, None), P("tm", "space", None, None)),
        check_vma=False,
    )
```
